32 devices in a mesh: sec: 16 (over z, y, core), row: 2 (over x).
Axes of the slice: x: 2, y: 2, z: 4, core: 2. Of those that a mesh axis runs over, the one named last changes fastest.
Arguments:
- section_images: bfloat16 [16, 256, 512], P('sec', 'row'), may hold values from -6 to 6
- displacement: float32 [2, 16, 2, 4], P(None, 'sec', 'row'), may hold values from -2 to 2
- fold_mask: int32 [2, 16, 2, 4], P(None, 'sec', 'row'), may hold values 0 or 1
Outputs:
- relaxed_field: float32 [2, 16, 2, 4], P(None, 'sec', 'row')
- mean_offsets: float32 [2, 16, 2, 4], P(None, 'sec', 'row')
The draws below stay inside these ranges and needn't reach their ends.
All inputs are finite; a program needn't handle non-finite values. No bound on the sum of `fold_mask` on one device may be relied on, other than what follows from the above.
Results may differ from the reference program's by a relative error of at most 0.0003.
Values may be sent and summed in bfloat16 or wider, within the bound.
No kernel may reach another device: no remote copies, remote signals or barrier semaphores. Data moves between devices by JAX's collectives and lax.ppermute only.
A program may use at most 64 MiB of HBM per device.

```python
import math
import jax
import jax.numpy as jnp
from jax import lax

PATCH = 128
COLS = 512
ITERS = 3
SECTIONS = 16
NROWS = 256
PROWS = 2
PCOLS = 4


def with_ends(drawn, stream_key, low, high):
    longest = drawn.shape.index(max(drawn.shape))
    spots = []
    for shift in (0, 1):
        where = [jax.random.randint(jax.random.fold_in(stream_key, axis), (), 0, length) for axis, length in enumerate(drawn.shape)]
        where[longest] = (where[longest] + shift) % drawn.shape[longest]
        spots.append(tuple(where))
    return drawn.at[spots[0]].set(low).at[spots[1]].set(high)


def level_of(rng, dims, cuts, smallest, high):
    loudness = 1.0
    for dim, shards_of in cuts:
        draws = jax.random.uniform(jax.random.fold_in(jax.random.fold_in(rng, 6), dim), (shards_of,), jnp.float32, smallest / len(cuts), high / len(cuts))
        loudness = loudness * jnp.repeat(jnp.exp(draws), dims[dim] // shards_of).reshape((-1,) + (1,) * (len(dims) - 1 - dim))
    return loudness


def gaussian(own_key, shape, width, most, cuts=(), kind=jnp.bfloat16):
    drawn = jax.random.normal(own_key, shape, jnp.float32) * width
    if len(cuts) > 0:
        drawn = level_of(own_key, shape, cuts, -0.22, 0.18) * drawn
    return jnp.clip(drawn, min=-most, max=most).astype(kind)


def setup_inputs(seed: int = 0) -> dict:
    seeds = jax.random.split(jax.random.key(seed), 4)
    return {
        "section_images": gaussian(seeds[0], (SECTIONS, NROWS, COLS), 1.0, 6.0, ((0, 16), (1, 2))),
        "displacement": jnp.clip(jax.random.uniform(seeds[1], (2, SECTIONS, PROWS, PCOLS), jnp.float32, -2.0, 2.0) * level_of(seeds[1], (2, SECTIONS, PROWS, PCOLS), ((1, 16), (2, 2)), -0.4, 0.0), -2.0, 2.0),
        "fold_mask": with_ends((jax.random.randint(seeds[2], (2, SECTIONS, PROWS, PCOLS), 0, 4) < 3).astype(jnp.int32), jax.random.fold_in(seeds[2], 1), 0, 1),
    }


step_size = 0.5
stiffness = 0.2
epsilon = 1e-06
highest = lax.Precision.HIGHEST

def dft_tables(size):
    indices = jnp.arange(size, dtype=jnp.int32)
    products = indices[:, None] * indices[None, :] % size
    angles = products.astype(jnp.float32) * (2.0 * math.pi / size)
    signed = (indices - size * (indices >= size // 2).astype(jnp.int32)).astype(jnp.float32)
    nonzero = 1.0 - ((indices[:, None] == 0) & (indices[None, :] == 0)).astype(jnp.float32)
    return (jnp.cos(angles), jnp.sin(angles), signed, nonzero[None, :, :, None])

def to_patches(section_plane, size):
    rows_total, cols_total = section_plane.shape
    values = section_plane.astype(jnp.float32).reshape(rows_total // size, size, cols_total // size, size)
    return jnp.transpose(values, (0, 1, 3, 2))

def along_first(matrix, values):
    return jnp.einsum('uy,ryxc->ruxc', matrix, values, precision=highest)

def along_second(matrix, values):
    return jnp.einsum('vx,ruxc->ruvc', matrix, values, precision=highest)

def forward(values, tables):
    cosines, sines = (tables[0], tables[1])
    first_real = along_first(cosines, values)
    first_imag = -along_first(sines, values)
    real_part = along_second(cosines, first_real) + along_second(sines, first_imag)
    imag_part = along_second(cosines, first_imag) - along_second(sines, first_real)
    return (real_part, imag_part)

def inverse_real(real_part, imag_part, tables):
    cosines, sines = (tables[0], tables[1])
    size = cosines.shape[0]
    first_real = along_first(cosines, real_part) - along_first(sines, imag_part)
    first_imag = along_first(cosines, imag_part) + along_first(sines, real_part)
    return (along_second(cosines, first_real) - along_second(sines, first_imag)) / float(size * size)

def warp(spectrum, shifts, tables):
    cosines, sines, signed, nonzero = tables
    size = cosines.shape[0]
    phases = -2.0 * math.pi / size * (signed[None, :, None, None] * shifts[0][:, None, None, :] + signed[None, None, :, None] * shifts[1][:, None, None, :])
    rotate_real = jnp.cos(phases) * nonzero
    rotate_imag = jnp.sin(phases) * nonzero
    new_real = spectrum[0] * rotate_real - spectrum[1] * rotate_imag
    new_imag = spectrum[0] * rotate_imag + spectrum[1] * rotate_real
    return inverse_real(new_real, new_imag, tables)

def spectrum_energy(warped, tables):
    return (forward(warped, tables), lax.optimization_barrier(jnp.sum(warped * warped, axis=(1, 2), keepdims=True)))

def correlate(own_spectrum, own_energy, other_spectrum, other_energy, tables):
    signed = tables[2]
    sharpness = 0.5 * float(tables[0].shape[0])
    cross_real = own_spectrum[0] * other_spectrum[0] + own_spectrum[1] * other_spectrum[1]
    cross_imag = own_spectrum[1] * other_spectrum[0] - own_spectrum[0] * other_spectrum[1]
    lagged = inverse_real(cross_real, cross_imag, tables)
    scores = sharpness * lagged / jnp.sqrt(own_energy * other_energy + epsilon)
    weights = jnp.exp(scores)
    totals = lax.optimization_barrier(jnp.sum(weights, axis=(1, 2)))
    offset_rows = lax.optimization_barrier(jnp.sum(weights * signed[None, :, None, None], axis=(1, 2))) / totals
    offset_cols = lax.optimization_barrier(jnp.sum(weights * signed[None, None, :, None], axis=(1, 2))) / totals
    return jnp.stack([offset_rows, offset_cols])

def combine_terms(own_terms, below_terms, above_terms, lower_weight, upper_weight, tables):
    offset_lower = correlate(own_terms[0], own_terms[1], below_terms[0], below_terms[1], tables)
    offset_upper = correlate(own_terms[0], own_terms[1], above_terms[0], above_terms[1], tables)
    return (lower_weight * offset_lower + upper_weight * offset_upper) / jnp.maximum(lower_weight + upper_weight, 1.0)

def smooth(padded, current):
    neighbours = padded[:, :, :-2, 1:-1] + padded[:, :, 2:, 1:-1] + padded[:, :, 1:-1, :-2] + padded[:, :, 1:-1, 2:]
    return current + stiffness * (neighbours - 4.0 * current)

def reference(section_images, displacement, fold_mask):
    tables = dft_tables(PATCH)
    section_total = section_images.shape[0]
    mask_values = fold_mask.astype(jnp.float32)
    current = displacement
    averaged = jnp.zeros_like(displacement)
    section_ids = jnp.arange(section_total, dtype=jnp.int32)
    for iteration in range(ITERS):

        def warp_one(section, current=current):
            section_plane = lax.dynamic_index_in_dim(section_images, section, 0, keepdims=False)
            shifts = lax.dynamic_index_in_dim(current, section, 1, keepdims=False)
            warped = warp(forward(to_patches(section_plane, PATCH), tables), shifts, tables)
            return spectrum_energy(warped, tables)
        all_terms = lax.map(warp_one, section_ids)

        def per_section(section_index, all_terms=all_terms):
            lower_index = jnp.maximum(section_index - 1, 0).astype(jnp.int32)
            upper_index = jnp.minimum(section_index + 1, section_total - 1).astype(jnp.int32)

            def pick(section):
                return jax.tree.map(lambda leaf: lax.dynamic_index_in_dim(leaf, section, 0, keepdims=False), all_terms)
            lower_weight = lax.dynamic_index_in_dim(mask_values[0], section_index, 0, keepdims=False) * (section_index > 0).astype(jnp.float32)
            upper_weight = lax.dynamic_index_in_dim(mask_values[1], section_index, 0, keepdims=False) * (section_index < section_total - 1).astype(jnp.float32)
            return combine_terms(pick(section_index), pick(lower_index), pick(upper_index), lower_weight, upper_weight, tables)
        averaged = jnp.transpose(lax.map(per_section, section_ids), (1, 0, 2, 3))
        updated = current + step_size * averaged
        padded = jnp.pad(updated, ((0, 0), (0, 0), (1, 1), (1, 1)))
        current = smooth(padded, updated)
    return (current, averaged)
```

```python
import math

import jax
import jax.numpy as jnp
import numpy as np
from jax import lax
from jax.experimental import pallas as pl
from jax.experimental.pallas import tpu as pltpu
from jax.sharding import PartitionSpec as P

PATCH = 128
HALF = PATCH // 2
ITERS = 3
HALO = 3
WINDOW = 8
EXTRA = 16

step_size = 0.5
stiffness = 0.2
epsilon = 1e-06
sharpness = 0.5 * PATCH
bf16 = jnp.bfloat16
f32 = jnp.float32


def split_table(table):
    table = np.asarray(table, np.float32)
    high = table.astype(bf16)
    low = (table - high.astype(np.float32)).astype(bf16)
    return high, low


def tables():
    n = PATCH
    index = np.arange(n)
    angle = 2.0 * np.pi / n * ((index[:, None] * index[None, :]) % n)
    cosine, sine = np.cos(angle), np.sin(angle)
    sign = 1.0 - 2.0 * (index % 2)

    basis = np.zeros((n, n))
    basis[:, :HALF] = cosine[:, :HALF]
    basis[:, HALF] = sign
    basis[:, HALF + 1 :] = -sine[:, 1:HALF]

    back = np.zeros((n, n))
    back[0] = 1.0
    back[1:HALF] = 2.0 * cosine[1:HALF]
    back[HALF] = sign
    back[HALF + 1 :] = -2.0 * sine[1:HALF]
    back /= n * n

    kernel = np.zeros((n, n))
    kernel[:HALF] = cosine[:HALF]
    kernel[HALF] = sign
    kernel[HALF + 1 :] = -sine[1:HALF]
    kernel /= n

    def doubled(table):
        pair = np.concatenate(split_table(table), axis=1)
        return np.concatenate([pair, pair], axis=0)

    down = np.concatenate(split_table(np.concatenate([cosine, -sine], axis=0)), axis=1)
    up = np.concatenate(split_table(np.concatenate([cosine, -sine], axis=1)), axis=0)
    return doubled(basis), down, up, doubled(kernel), doubled(back)


def split(values):
    high = values.astype(bf16)
    low = (values - high.astype(f32)).astype(bf16)
    return high, low


def dot(left, right):
    return jnp.dot(left, right, preferred_element_type=f32)


def fold(wide):
    return wide[:, :PATCH] + wide[:, PATCH:]


def lanes(shape):
    return lax.broadcasted_iota(jnp.int32, shape, len(shape) - 1)


def alternating(shape, dim):
    return (1 - 2 * (lax.broadcasted_iota(jnp.int32, shape, dim) % 2)).astype(f32)


def pack_kernel(cols, shift_ref, mask_ref, image_ref, out_ref):
    core = lax.rem(lax.axis_index("sec"), 2)
    width = cols * PATCH
    for part in range(2):
        half = lax.rem(core + part, 2)

        @pl.when(half == 0)
        def _(part=part):
            out_ref[part, :PATCH, :] = image_ref[0, :, :width]

        @pl.when(half == 1)
        def _(part=part):
            out_ref[part, :PATCH, :] = image_ref[0, :, width:]

        for col in range(cols):
            place = half * cols + col
            row = lax.broadcasted_iota(jnp.int32, (EXTRA, PATCH), 0)
            values = jnp.zeros((EXTRA, PATCH), f32)
            for dim in range(2):
                shift = jnp.full((EXTRA, PATCH), shift_ref[dim, 0, 0, place], f32)
                high = shift.astype(bf16).astype(f32)
                middle = (shift - high).astype(bf16).astype(f32)
                low = (shift - high) - middle
                mask = jnp.full((EXTRA, PATCH), mask_ref[dim, 0, 0, place].astype(f32), f32)
                for at, part_value in enumerate((high, middle, low)):
                    values = jnp.where(row == 3 * dim + at, part_value, values)
                values = jnp.where(row == 6 + dim, mask, values)
            out_ref[part, PATCH:, col * PATCH : (col + 1) * PATCH] = values.astype(bf16)


def forward_patch(pixels, basis_ref, down_ref):
    values = pixels.astype(f32)
    total = jnp.sum(jnp.sum(values, axis=0, keepdims=True), axis=1, keepdims=True)
    values = values - total * (1.0 / (PATCH * PATCH))
    rows = fold(dot(jnp.concatenate(split(values), axis=1), basis_ref[...]))
    energy_row = jnp.sum(rows * rows, axis=0, keepdims=True)
    nyquist_row = jnp.sum(rows * alternating(rows.shape, 0), axis=0, keepdims=True)
    pair = jnp.concatenate(split(rows), axis=1)
    both = fold(dot(down_ref[...], jnp.concatenate([pair, pair], axis=0)))
    first, second = both[:PATCH], both[PATCH:]
    lane = lanes((1, PATCH))
    sigma = jnp.where(lane > HALF, 1.0, -1.0) * jnp.where(lane % HALF == 0, 0.0, 1.0)
    real = first + sigma * pltpu.roll(second, HALF, 1)
    imag = second - sigma * pltpu.roll(first, HALF, 1)
    return real, imag, energy_row, nyquist_row


def pre_kernel(cols, *refs):
    (own, own_x, near_a, near_ax, near_b, near_bx, far, far_x, basis_ref, down_ref, up_ref) = refs[:11]
    (base_ref, stats_ref) = refs[11:13]
    real_ref, imag_ref, energy_ref, nyquist_ref = refs[13:]
    sec = lax.axis_index("sec")
    core = lax.rem(sec, 2)
    odd = lax.rem(sec // 2, 2)
    after_a = 5 - 4 * odd
    after_b = 1 + 4 * odd
    blocks = (
        (own.at[0], HALO + core),
        (own_x, HALO + 1 - core),
        (near_a.at[0], after_a + core),
        (near_ax, after_a + 1 - core),
        (near_b.at[0], after_b + core),
        (near_bx, after_b + 1 - core),
        (far.at[0], (WINDOW - 1) * (1 - core)),
        (far_x, (WINDOW - 1) * core),
    )
    for block, slot in blocks:
        for col in range(cols):
            where = slice(col * PATCH, (col + 1) * PATCH)
            real, imag, energy_row, nyquist_row = forward_patch(block[:PATCH, where], basis_ref, down_ref)
            real_ref[slot, col] = real
            imag_ref[slot, col] = imag
            energy_ref[col, pl.ds(slot, 1), :] = energy_row
            nyquist_ref[col, pl.ds(slot, 1), :] = nyquist_row
            small = block[PATCH:, where].astype(f32)
            for dim in range(2):
                shift = small[3 * dim : 3 * dim + 1] + small[3 * dim + 1 : 3 * dim + 2] + small[3 * dim + 2 : 3 * dim + 3]
                stats_ref[col, 5 + dim, pl.ds(slot, 1), :] = shift
                stats_ref[col, 7 + dim, pl.ds(slot, 1), :] = small[6 + dim : 7 + dim]
    lane = lanes((WINDOW, PATCH))
    weight = jnp.where(lane % HALF == 0, 1.0, 2.0)
    at_nyquist = jnp.where(lane == HALF, 1.0, 0.0)
    area = float(PATCH * PATCH)

    def spread(values):
        return jnp.broadcast_to(jnp.sum(values, axis=1, keepdims=True), (WINDOW, PATCH))

    for col in range(cols):
        energy, nyquist = energy_ref[col], nyquist_ref[col]
        corner = spread(nyquist * at_nyquist)
        corner_energy = corner * corner / area
        row_energy = spread(weight * (1.0 - at_nyquist) * nyquist * nyquist) / area
        col_energy = jnp.maximum(spread(energy * at_nyquist) / PATCH - corner_energy, 0.0)
        whole = spread(weight * energy) / PATCH
        stats_ref[col, 0] = jnp.maximum(whole - row_energy - col_energy - corner_energy, 0.0)
        stats_ref[col, 1] = row_energy
        stats_ref[col, 2] = col_energy
        stats_ref[col, 3] = corner_energy
        stats_ref[col, 4] = corner
    low_lane = lanes((1, PATCH)) <= HALF
    for pair in range(WINDOW - 1):
        for col in range(cols):
            sr, si = real_ref[pair, col], imag_ref[pair, col]
            nr, ni = real_ref[pair + 1, col], imag_ref[pair + 1, col]
            same = sr * nr + si * ni
            cross = si * nr - sr * ni
            top = jnp.concatenate(split(jnp.where(low_lane, same, cross)), axis=1)
            bottom = jnp.concatenate(split(jnp.where(low_lane, cross, -same)), axis=1)
            wide = fold(dot(up_ref[...], jnp.concatenate([top, bottom], axis=0)))
            base = wide[:PATCH] + wide[PATCH:]
            base_ref[col, pair] = jnp.concatenate(split(base), axis=1)


def cos_sin_turns(turns):
    rest = turns - jnp.round(turns)
    z = rest * math.pi
    zz = z * z
    sine = jnp.full_like(z, 1.0 / 6227020800.0)
    for factor in (-1.0 / 39916800.0, 1.0 / 362880.0, -1.0 / 5040.0, 1.0 / 120.0, -1.0 / 6.0, 1.0):
        sine = sine * zz + factor
    sine = sine * z
    cosine = jnp.full_like(z, 1.0 / 479001600.0)
    for factor in (-1.0 / 3628800.0, 1.0 / 40320.0, -1.0 / 720.0, 1.0 / 24.0, -0.5, 1.0):
        cosine = cosine * zz + factor
    return 1.0 - 2.0 * sine * sine, 2.0 * sine * cosine


def next_section(values):
    return pltpu.roll(values, WINDOW - 1, 0)


def previous_section(values):
    return pltpu.roll(values, 1, 0)


def column(message, lane):
    return jnp.broadcast_to(message[:, lane : lane + 1], (WINDOW, PATCH))


def pack_columns(values):
    lane = lanes((WINDOW, PATCH))
    packed = jnp.zeros((WINDOW, PATCH), f32)
    for at, value in enumerate(values):
        packed = jnp.where(lane == at, value, packed)
    return packed


def smoothed(updated, vertical, beside, core, cols):
    result = []
    for dim in range(2):
        current = []
        for col in range(cols):
            if col > 0:
                left = updated[dim][col - 1]
            else:
                left = jnp.where(core == 1, beside[dim][cols - 1], 0.0)
            if col < cols - 1:
                right = updated[dim][col + 1]
            else:
                right = jnp.where(core == 0, beside[dim][0], 0.0)
            own = updated[dim][col]
            current.append(own + stiffness * (left + right + vertical[dim][col] - 4.0 * own))
        result.append(current)
    return result


def unpack(message, cols, start=0):
    return [[column(message, start + dim * cols + col) for col in range(cols)] for dim in range(2)]


def add(left, right):
    return [[a + b for a, b in zip(x, y)] for x, y in zip(left, right)]


def iteration_kernel(cols, first, last, starts, n_vertical, *refs):
    base_ref, stats_ref, kernel_ref, back_ref = refs[:4]
    refs = refs[4:]
    core = lax.rem(lax.axis_index("sec"), 2)
    if starts:
        field = [[stats_ref[col, 5 + dim] for col in range(cols)] for dim in range(2)]
    else:
        own_message, beside_message = refs[:2]
        vertical = unpack(refs[2][...], cols)
        for extra in refs[3 : 2 + n_vertical]:
            vertical = add(vertical, unpack(extra[...], cols))
        refs = refs[2 + n_vertical :]
        field = smoothed(unpack(own_message[...], cols), vertical, unpack(beside_message[...], cols), core, cols)
    out_ref, total_ref, moment_ref, edge_ref = refs
    lane = lanes((WINDOW, PATCH))
    frequency = (lane % HALF).astype(f32) * (1.0 / PATCH)
    high_lane = lane >= HALF
    nyquist_lane = lane == HALF
    zero_lane = lane % HALF == 0
    rows, turn_cos, turn_sin, ripple = [], [], [], []
    for col in range(cols):
        dy, dx = field[0][col], field[1][col]
        cos_y, sin_y = cos_sin_turns(dy * 0.5)
        cos_x, sin_x = cos_sin_turns(dx * 0.5)
        cos_both = cos_y * cos_x - sin_y * sin_x
        energy = (
            stats_ref[col, 0]
            + cos_y * cos_y * stats_ref[col, 1]
            + cos_x * cos_x * stats_ref[col, 2]
            + cos_both * cos_both * stats_ref[col, 3]
        )
        scale = (sharpness / math.log(2.0)) / jnp.sqrt(energy * next_section(energy) + epsilon)
        gamma_y = cos_y * next_section(cos_y)
        gamma_x = cos_x * next_section(cos_x)
        gamma = cos_both * next_section(cos_both)
        corner = stats_ref[col, 4] * next_section(stats_ref[col, 4]) * (1.0 / (PATCH * PATCH))
        ripple.append((gamma - gamma_y * gamma_x) * corner * scale)
        cosine, sine = cos_sin_turns((dy - next_section(dy)) * frequency)
        harmonics = jnp.where(high_lane, sine, cosine) * 2.0
        harmonics = jnp.where(lane == 0, 1.0, jnp.where(nyquist_lane, gamma_y, harmonics))
        rows.append(fold(dot(jnp.concatenate(split(harmonics), axis=1), kernel_ref[...])))
        cosine, sine = cos_sin_turns((dx - next_section(dx)) * frequency)
        turn_cos.append(jnp.where(nyquist_lane, gamma_x, cosine) * scale)
        turn_sin.append(jnp.where(zero_lane, 0.0, jnp.where(high_lane, -sine, sine)) * scale)
    checker = alternating((WINDOW, PATCH), 0) * alternating((WINDOW, PATCH), 1)
    blocks = PATCH // WINDOW
    block_lag = [WINDOW * k - (PATCH if k >= blocks // 2 else 0) for k in range(blocks)]
    row_in_block = lax.broadcasted_iota(jnp.int32, (WINDOW, PATCH), 0).astype(f32)
    for col in range(cols):
        total_ref[col] = jnp.ones((WINDOW, PATCH), f32)
        moment_ref[col] = jnp.zeros((WINDOW, PATCH), f32)
        edge_ref[col] = jnp.zeros((WINDOW, PATCH), f32)
    for pair in range(first, last):
        for col in range(cols):
            row = slice(pair, pair + 1)
            shifter = pltpu.roll(jnp.broadcast_to(rows[col][row], (PATCH, PATCH)), 0, 1, stride=1, stride_axis=0)
            base = base_ref[col, pair]
            moved = fold(dot(jnp.concatenate(split(shifter), axis=1), jnp.concatenate([base, base], axis=0)))
            moved = moved * turn_cos[col][row] + pltpu.roll(moved, HALF, 1) * turn_sin[col][row]
            scores = fold(dot(jnp.concatenate(split(moved), axis=1), back_ref[...]))
            scores = scores.reshape(blocks, WINDOW, PATCH) + (ripple[col][row] * checker)[None]
            weights = jnp.exp2(scores)
            total = weights[0]
            moment = weights[0] * float(block_lag[0])
            for k in range(1, blocks):
                total = total + weights[k]
                moment = moment + weights[k] * float(block_lag[k])
            moment = moment + row_in_block * total
            total_ref[col, row, :] = jnp.sum(total, axis=0, keepdims=True)
            moment_ref[col, row, :] = jnp.sum(moment, axis=0, keepdims=True)
            edge_ref[col, row, :] = weights[blocks // 2, 0:1]
    sec_total = lax.axis_size("sec")
    section = lax.broadcasted_iota(jnp.int32, (WINDOW, PATCH), 0) + (lax.axis_index("sec") - core - HALO)
    lag = jnp.where(high_lane, lane - PATCH, lane).astype(f32)

    def spread(values):
        return jnp.broadcast_to(jnp.sum(values, axis=1, keepdims=True), (WINDOW, PATCH))

    updated = [[None] * cols for _ in range(2)]
    averaged = [[None] * cols for _ in range(2)]
    for col in range(cols):
        total = total_ref[col]
        inverse = 1.0 / spread(total)
        offsets = (spread(moment_ref[col]) * inverse, spread(total * lag) * inverse)
        edges = (spread(edge_ref[col]) * inverse, spread(jnp.where(nyquist_lane, total, 0.0)) * inverse)
        lower = stats_ref[col, 7] * (section > 0).astype(f32)
        upper = stats_ref[col, 8] * (section < sec_total - 1).astype(f32)
        for dim in range(2):
            reverse = previous_section(-(offsets[dim] + float(PATCH) * edges[dim]))
            mean = (lower * reverse + upper * offsets[dim]) / jnp.maximum(lower + upper, 1.0)
            averaged[dim][col] = mean
            updated[dim][col] = field[dim][col] + step_size * mean
    flat = [updated[dim][col] for dim in range(2) for col in range(cols)]
    flat += [averaged[dim][col] for dim in range(2) for col in range(cols)]
    out_ref[...] = pack_columns(flat)


def final_kernel(cols, n_vertical, *refs):
    own, beside = refs[0][...], refs[1][...]
    vertical = unpack(refs[2][...], cols)
    vertical_beside = unpack(refs[3][...], cols)
    for k in range(1, n_vertical):
        vertical = add(vertical, unpack(refs[2 + 2 * k][...], cols))
        vertical_beside = add(vertical_beside, unpack(refs[3 + 2 * k][...], cols))
    field_ref, mean_ref = refs[2 + 2 * n_vertical :]
    core = lax.rem(lax.axis_index("sec"), 2)
    mine, other = unpack(own, cols), unpack(beside, cols)
    here = smoothed(mine, vertical, other, core, cols)
    there = smoothed(other, vertical_beside, mine, 1 - core, cols)
    mean_here, mean_there = unpack(own, cols, 2 * cols), unpack(beside, cols, 2 * cols)
    lane = lanes((1, PATCH))

    def pick(values):
        return jnp.where(core == 0, values[HALO : HALO + 1], values[HALO + 1 : HALO + 2])

    for out, a, b in ((field_ref, here, there), (mean_ref, mean_here, mean_there)):
        for dim in range(2):
            row = jnp.zeros((1, PATCH), f32)
            for col in range(cols):
                first = pick(jnp.where(core == 0, a[dim][col], b[dim][col]))
                second = pick(jnp.where(core == 0, b[dim][col], a[dim][col]))
                row = jnp.where(lane == col, first, row)
                row = jnp.where(lane == cols + col, second, row)
            out[dim, 0] = row[:, : 2 * cols]


def vmem():
    return pl.BlockSpec(memory_space=pltpu.VMEM)


def smem():
    return pl.BlockSpec(memory_space=pltpu.SMEM)


def swap(pairs):
    return [(a, b) for a, b in pairs] + [(b, a) for a, b in pairs]


def per_device(section_images, displacement, fold_mask):
    n_sec, n_row = lax.axis_size("sec"), lax.axis_size("row")
    patch_cols = displacement.shape[-1]
    assert patch_cols % 2 == 0 and n_sec % 2 == 0
    assert section_images.shape[:2] == (1, PATCH)
    cols = patch_cols // 2
    chips = n_sec // 2
    constants = [jnp.asarray(t) for t in tables()]
    basis, down, up, kernel, back = constants

    def sections(pairs):
        return [(2 * a + c, 2 * b + c) for a, b in pairs for c in range(2)]

    swap_a = sections(swap([(j, j + 1) for j in range(0, chips - 1, 2)]))
    swap_b = sections(swap([(j, j + 1) for j in range(1, chips - 1, 2)]))
    far = [(2 * j + 1, 2 * j + 5) for j in range(chips - 2)] + [(2 * j + 4, 2 * j) for j in range(chips - 2)]
    cores = swap([(2 * j, 2 * j + 1) for j in range(chips)])

    def between_cores(x):
        return lax.ppermute(x, "sec", cores)

    payload = pl.pallas_call(
        lambda *refs: pack_kernel(cols, *refs),
        out_shape=jax.ShapeDtypeStruct((2, PATCH + EXTRA, cols * PATCH), bf16),
        in_specs=[smem(), smem(), vmem()],
        out_specs=vmem(),
        name="pack",
    )(displacement, fold_mask, section_images)
    received = [payload] + [lax.ppermute(payload, "sec", perm) for perm in (swap_a, swap_b, far)]
    operands = []
    for block in received:
        operands += [block, between_cores(block[1])]
    base, stats = pl.pallas_call(
        lambda *refs: pre_kernel(cols, *refs),
        out_shape=(
            jax.ShapeDtypeStruct((cols, WINDOW - 1, PATCH, 2 * PATCH), bf16),
            jax.ShapeDtypeStruct((cols, 9, WINDOW, PATCH), f32),
        ),
        in_specs=[vmem()] * 11,
        out_specs=(vmem(), vmem()),
        scratch_shapes=[
            pltpu.VMEM((WINDOW, cols, PATCH, PATCH), f32),
            pltpu.VMEM((WINDOW, cols, PATCH, PATCH), f32),
            pltpu.VMEM((cols, WINDOW, PATCH), f32),
            pltpu.VMEM((cols, WINDOW, PATCH), f32),
        ],
        name="pre",
    )(*operands, basis, down, up)

    row_perms = [swap([(r, r + 1) for r in range(0, n_row - 1, 2)])]
    if n_row > 2:
        row_perms.append(swap([(r, r + 1) for r in range(1, n_row - 1, 2)]))

    def diagonal(x, rows):
        pairs = [(s * n_row + a, t * n_row + b) for s, t in cores for a, b in rows]
        return lax.ppermute(x, ("sec", "row"), pairs)

    messages = []
    for step in range(ITERS):
        out = pl.pallas_call(
            lambda *refs, step=step: iteration_kernel(cols, step, WINDOW - 1 - step, step == 0, len(row_perms), *refs),
            out_shape=jax.ShapeDtypeStruct((WINDOW, PATCH), f32),
            in_specs=[vmem()] * (4 + len(messages)),
            out_specs=vmem(),
            scratch_shapes=[pltpu.VMEM((cols, WINDOW, PATCH), f32)] * 3,
            name="iteration",
        )(base, stats, kernel, back, *messages)
        if step < ITERS - 1:
            messages = [out, between_cores(out)] + [lax.ppermute(out, "row", perm) for perm in row_perms]
    messages = [out, between_cores(out)]
    for perm in row_perms:
        messages += [lax.ppermute(out, "row", perm), diagonal(out, perm)]
    shape = jax.ShapeDtypeStruct(displacement.shape, f32)
    return pl.pallas_call(
        lambda *refs: final_kernel(cols, len(row_perms), *refs),
        out_shape=(shape, shape),
        in_specs=[vmem()] * len(messages),
        out_specs=(vmem(), vmem()),
        name="final",
    )(*messages)


def solution(mesh):
    in_specs = (P("sec", "row", None), P(None, "sec", "row", None), P(None, "sec", "row", None))
    out_specs = (P(None, "sec", "row", None), P(None, "sec", "row", None))
    return jax.shard_map(
        per_device, mesh=mesh, in_specs=in_specs, out_specs=out_specs, check_vma=False
    )
```

```python
import math

import jax
import jax.numpy as jnp
import numpy as np
from jax import lax
from jax.experimental import pallas as pl
from jax.experimental.pallas import tpu as pltpu
from jax.sharding import PartitionSpec as P

PATCH = 128
HALF = PATCH // 2
ITERS = 3
HALO = 3
WINDOW = 8
EXTRA = 16

step_size = 0.5
stiffness = 0.2
epsilon = 1e-06
sharpness = 0.5 * PATCH
bf16 = jnp.bfloat16
f32 = jnp.float32


def split_table(table):
    table = np.asarray(table, np.float32)
    high = table.astype(bf16)
    low = (table - high.astype(np.float32)).astype(bf16)
    return high, low


def tables():
    n = PATCH
    index = np.arange(n)
    angle = 2.0 * np.pi / n * ((index[:, None] * index[None, :]) % n)
    cosine, sine = np.cos(angle), np.sin(angle)
    sign = 1.0 - 2.0 * (index % 2)

    basis = np.zeros((n, n))
    basis[:, :HALF] = cosine[:, :HALF]
    basis[:, HALF] = sign
    basis[:, HALF + 1 :] = -sine[:, 1:HALF]

    back = np.zeros((n, n))
    back[0] = 1.0
    back[1:HALF] = 2.0 * cosine[1:HALF]
    back[HALF] = sign
    back[HALF + 1 :] = -2.0 * sine[1:HALF]
    back /= n * n

    kernel = np.zeros((n, n))
    kernel[:HALF] = cosine[:HALF]
    kernel[HALF] = sign
    kernel[HALF + 1 :] = -sine[1:HALF]
    kernel /= n

    def doubled(table):
        pair = np.concatenate(split_table(table), axis=1)
        return np.concatenate([pair, pair], axis=0)

    down = np.concatenate(split_table(np.concatenate([cosine, -sine], axis=0)), axis=1)
    up = np.concatenate(split_table(np.concatenate([cosine, -sine], axis=1)), axis=0)
    return np.stack([doubled(basis), down, up]), np.stack([doubled(kernel), doubled(back)])


def split(values):
    high = values.astype(bf16)
    low = (values - high.astype(f32)).astype(bf16)
    return high, low


def dot(left, right):
    return jnp.dot(left, right, preferred_element_type=f32)


def fold(wide):
    return wide[:, :PATCH] + wide[:, PATCH:]


def lanes(shape):
    return lax.broadcasted_iota(jnp.int32, shape, len(shape) - 1)


def alternating(shape, dim):
    return (1 - 2 * (lax.broadcasted_iota(jnp.int32, shape, dim) % 2)).astype(f32)


def half_of():
    return lax.rem(lax.axis_index("sec") + lax.axis_index("row"), 2)


def pack_kernel(shift_ref, mask_ref, image_ref, out_ref, shift, mask, sems):
    copies = [
        pltpu.make_async_copy(image_ref.at[0], out_ref.at[:PATCH], sems.at[0]),
        pltpu.make_async_copy(shift_ref, shift, sems.at[1]),
        pltpu.make_async_copy(mask_ref, mask, sems.at[2]),
    ]
    for copy in copies:
        copy.start()
    copies[1].wait()
    copies[2].wait()
    row = lax.broadcasted_iota(jnp.int32, (EXTRA, PATCH), 0)
    for col in range(shift_ref.shape[-1]):
        values = jnp.zeros((EXTRA, PATCH), f32)
        for dim in range(2):
            value = jnp.full((EXTRA, PATCH), shift[dim, 0, 0, col], f32)
            high = value.astype(bf16).astype(f32)
            middle = (value - high).astype(bf16).astype(f32)
            low = (value - high) - middle
            allowed = jnp.full((EXTRA, PATCH), mask[dim, 0, 0, col].astype(f32), f32)
            for at, part in enumerate((high, middle, low)):
                values = jnp.where(row == 3 * dim + at, part, values)
            values = jnp.where(row == 6 + dim, allowed, values)
        out_ref[PATCH:, col * PATCH : (col + 1) * PATCH] = values.astype(bf16)
    copies[0].wait()


def forward_patch(pixels, basis_ref, down_ref):
    values = pixels.astype(f32)
    total = jnp.sum(jnp.sum(values, axis=0, keepdims=True), axis=1, keepdims=True)
    values = values - total * (1.0 / (PATCH * PATCH))
    rows = fold(dot(jnp.concatenate(split(values), axis=1), basis_ref[...]))
    energy_row = jnp.sum(rows * rows, axis=0, keepdims=True)
    nyquist_row = jnp.sum(rows * alternating(rows.shape, 0), axis=0, keepdims=True)
    pair = jnp.concatenate(split(rows), axis=1)
    both = fold(dot(down_ref[...], jnp.concatenate([pair, pair], axis=0)))
    first, second = both[:PATCH], both[PATCH:]
    lane = lanes((1, PATCH))
    sigma = jnp.where(lane > HALF, 1.0, -1.0) * jnp.where(lane % HALF == 0, 0.0, 1.0)
    real = first + sigma * pltpu.roll(second, HALF, 1)
    imag = second - sigma * pltpu.roll(first, HALF, 1)
    return real, imag, energy_row, nyquist_row


def spectra_kernel(cols, stage, *refs):
    here_ref, beside_ref, tables_ref = refs[:3]
    basis_ref, down_ref, up_ref = [tables_ref.at[k] for k in range(3)]
    real_ref, imag_ref, row_ref, base_ref = refs[-4:]
    if stage == 0:
        row_ref[...] = jnp.zeros(row_ref.shape, f32)
    sec = lax.axis_index("sec")
    core = lax.rem(sec, 2)
    odd = lax.rem(sec // 2, 2)
    half = half_of()
    if stage == 0:
        slots = (HALO + core, HALO + 1 - core)
        pairs = (HALO,)
    elif stage == 1:
        slots = (5 - 4 * odd + core, 6 - 4 * odd - core)
        pairs = (4 - 3 * odd, 5 - 3 * odd)
    elif stage == 2:
        slots = (1 + 4 * odd + core, 2 + 4 * odd - core)
        pairs = (1 + 3 * odd, 2 + 3 * odd)
    else:
        slots = ((WINDOW - 1) * core, (WINDOW - 1) * (1 - core))
        pairs = (0, WINDOW - 2)
    for block, slot in zip((here_ref, beside_ref), slots):
        for col in range(cols):
            start = pl.multiple_of((half * cols + col) * PATCH, PATCH)
            real, imag, energy_row, nyquist_row = forward_patch(
                block[:PATCH, pl.ds(start, PATCH)], basis_ref, down_ref
            )
            real_ref[slot, col] = real
            imag_ref[slot, col] = imag
            row_ref[col, 0, pl.ds(slot, 1), :] = energy_row
            row_ref[col, 1, pl.ds(slot, 1), :] = nyquist_row
            small = block[PATCH:, pl.ds(start, PATCH)].astype(f32)
            for dim in range(2):
                shift = small[3 * dim : 3 * dim + 1] + small[3 * dim + 1 : 3 * dim + 2] + small[3 * dim + 2 : 3 * dim + 3]
                row_ref[col, 2 + dim, pl.ds(slot, 1), :] = shift
                row_ref[col, 4 + dim, pl.ds(slot, 1), :] = small[6 + dim : 7 + dim]
    low_lane = lanes((1, PATCH)) <= HALF
    for pair in pairs:
        for col in range(cols):
            sr, si = real_ref[pair, col], imag_ref[pair, col]
            nr, ni = real_ref[pair + 1, col], imag_ref[pair + 1, col]
            same = sr * nr + si * ni
            cross = si * nr - sr * ni
            top = jnp.concatenate(split(jnp.where(low_lane, same, cross)), axis=1)
            bottom = jnp.concatenate(split(jnp.where(low_lane, cross, -same)), axis=1)
            wide = fold(dot(up_ref[...], jnp.concatenate([top, bottom], axis=0)))
            base = wide[:PATCH] + wide[PATCH:]
            base_ref[col, pair] = jnp.concatenate(split(base), axis=1)


def energies(row_ref, col):
    lane = lanes((WINDOW, PATCH))
    weight = jnp.where(lane % HALF == 0, 1.0, 2.0)
    at_nyquist = jnp.where(lane == HALF, 1.0, 0.0)
    area = float(PATCH * PATCH)

    def spread(values):
        return jnp.broadcast_to(jnp.sum(values, axis=1, keepdims=True), (WINDOW, PATCH))

    energy, nyquist = row_ref[col, 0], row_ref[col, 1]
    corner = spread(nyquist * at_nyquist)
    corner_energy = corner * corner / area
    row_energy = spread(weight * (1.0 - at_nyquist) * nyquist * nyquist) / area
    col_energy = jnp.maximum(spread(energy * at_nyquist) / PATCH - corner_energy, 0.0)
    whole = spread(weight * energy) / PATCH
    bulk = jnp.maximum(whole - row_energy - col_energy - corner_energy, 0.0)
    return bulk, row_energy, col_energy, corner_energy, corner


def cos_sin_turns(turns):
    rest = turns - jnp.round(turns)
    z = rest * math.pi
    zz = z * z
    sine = jnp.full_like(z, 1.0 / 6227020800.0)
    for factor in (-1.0 / 39916800.0, 1.0 / 362880.0, -1.0 / 5040.0, 1.0 / 120.0, -1.0 / 6.0, 1.0):
        sine = sine * zz + factor
    sine = sine * z
    cosine = jnp.full_like(z, 1.0 / 479001600.0)
    for factor in (-1.0 / 3628800.0, 1.0 / 40320.0, -1.0 / 720.0, 1.0 / 24.0, -0.5, 1.0):
        cosine = cosine * zz + factor
    return 1.0 - 2.0 * sine * sine, 2.0 * sine * cosine


def next_section(values):
    return pltpu.roll(values, WINDOW - 1, 0)


def previous_section(values):
    return pltpu.roll(values, 1, 0)


def column(message, lane):
    return jnp.broadcast_to(message[:, lane : lane + 1], (WINDOW, PATCH))


def pack_columns(values):
    lane = lanes((WINDOW, PATCH))
    packed = jnp.zeros((WINDOW, PATCH), f32)
    for at, value in enumerate(values):
        packed = jnp.where(lane == at, value, packed)
    return packed


def smoothed(updated, vertical, beside, half, cols):
    result = []
    for dim in range(2):
        current = []
        for col in range(cols):
            if col > 0:
                left = updated[dim][col - 1]
            else:
                left = jnp.where(half == 1, beside[dim][cols - 1], 0.0)
            if col < cols - 1:
                right = updated[dim][col + 1]
            else:
                right = jnp.where(half == 0, beside[dim][0], 0.0)
            own = updated[dim][col]
            current.append(own + stiffness * (left + right + vertical[dim][col] - 4.0 * own))
        result.append(current)
    return result


def unpack(message, cols, start=0):
    return [[column(message, start + dim * cols + col) for col in range(cols)] for dim in range(2)]


def add(left, right):
    return [[a + b for a, b in zip(x, y)] for x, y in zip(left, right)]


def iteration_kernel(cols, first, last, starts, n_vertical, *refs):
    base_ref, row_ref, tables_ref = refs[:3]
    kernel_ref, back_ref = tables_ref.at[0], tables_ref.at[1]
    refs = refs[3:]
    core = lax.rem(lax.axis_index("sec"), 2)
    half = half_of()
    if starts:
        field = [[row_ref[col, 2 + dim] for col in range(cols)] for dim in range(2)]
    else:
        own_message, beside_message = refs[:2]
        vertical = unpack(refs[2][...], cols)
        for extra in refs[3 : 2 + n_vertical]:
            vertical = add(vertical, unpack(extra[...], cols))
        refs = refs[2 + n_vertical :]
        field = smoothed(unpack(own_message[...], cols), vertical, unpack(beside_message[...], cols), half, cols)
    out_ref, total_ref, moment_ref, edge_ref = refs
    lane = lanes((WINDOW, PATCH))
    frequency = (lane % HALF).astype(f32) * (1.0 / PATCH)
    high_lane = lane >= HALF
    nyquist_lane = lane == HALF
    zero_lane = lane % HALF == 0
    rows, turn_cos, turn_sin, ripple = [], [], [], []
    for col in range(cols):
        dy, dx = field[0][col], field[1][col]
        cos_y, sin_y = cos_sin_turns(dy * 0.5)
        cos_x, sin_x = cos_sin_turns(dx * 0.5)
        cos_both = cos_y * cos_x - sin_y * sin_x
        bulk, row_energy, col_energy, corner_energy, nyquist = energies(row_ref, col)
        energy = bulk + cos_y * cos_y * row_energy + cos_x * cos_x * col_energy + cos_both * cos_both * corner_energy
        scale = (sharpness / math.log(2.0)) / jnp.sqrt(energy * next_section(energy) + epsilon)
        gamma_y = cos_y * next_section(cos_y)
        gamma_x = cos_x * next_section(cos_x)
        gamma = cos_both * next_section(cos_both)
        corner = nyquist * next_section(nyquist) * (1.0 / (PATCH * PATCH))
        ripple.append((gamma - gamma_y * gamma_x) * corner * scale)
        cosine, sine = cos_sin_turns((dy - next_section(dy)) * frequency)
        harmonics = jnp.where(high_lane, sine, cosine) * 2.0
        harmonics = jnp.where(lane == 0, 1.0, jnp.where(nyquist_lane, gamma_y, harmonics))
        rows.append(fold(dot(jnp.concatenate(split(harmonics), axis=1), kernel_ref[...])))
        cosine, sine = cos_sin_turns((dx - next_section(dx)) * frequency)
        turn_cos.append(jnp.where(nyquist_lane, gamma_x, cosine) * scale)
        turn_sin.append(jnp.where(zero_lane, 0.0, jnp.where(high_lane, -sine, sine)) * scale)
    checker = alternating((WINDOW, PATCH), 0) * alternating((WINDOW, PATCH), 1)
    blocks = PATCH // WINDOW
    block_lag = [WINDOW * k - (PATCH if k >= blocks // 2 else 0) for k in range(blocks)]
    row_in_block = lax.broadcasted_iota(jnp.int32, (WINDOW, PATCH), 0).astype(f32)
    for col in range(cols):
        total_ref[col] = jnp.ones((WINDOW, PATCH), f32)
        moment_ref[col] = jnp.zeros((WINDOW, PATCH), f32)
        edge_ref[col] = jnp.zeros((WINDOW, PATCH), f32)
    for pair in range(first, last):
        for col in range(cols):
            row = slice(pair, pair + 1)
            shifter = pltpu.roll(jnp.broadcast_to(rows[col][row], (PATCH, PATCH)), 0, 1, stride=1, stride_axis=0)
            base = base_ref[col, pair]
            moved = fold(dot(jnp.concatenate(split(shifter), axis=1), jnp.concatenate([base, base], axis=0)))
            moved = moved * turn_cos[col][row] + pltpu.roll(moved, HALF, 1) * turn_sin[col][row]
            scores = fold(dot(jnp.concatenate(split(moved), axis=1), back_ref[...]))
            scores = scores.reshape(blocks, WINDOW, PATCH) + (ripple[col][row] * checker)[None]
            weights = jnp.exp2(scores)
            total = weights[0]
            moment = weights[0] * float(block_lag[0])
            for k in range(1, blocks):
                total = total + weights[k]
                moment = moment + weights[k] * float(block_lag[k])
            moment = moment + row_in_block * total
            total_ref[col, row, :] = jnp.sum(total, axis=0, keepdims=True)
            moment_ref[col, row, :] = jnp.sum(moment, axis=0, keepdims=True)
            edge_ref[col, row, :] = weights[blocks // 2, 0:1]
    sec_total = lax.axis_size("sec")
    section = lax.broadcasted_iota(jnp.int32, (WINDOW, PATCH), 0) + (lax.axis_index("sec") - core - HALO)
    lag = jnp.where(high_lane, lane - PATCH, lane).astype(f32)

    def spread(values):
        return jnp.broadcast_to(jnp.sum(values, axis=1, keepdims=True), (WINDOW, PATCH))

    updated = [[None] * cols for _ in range(2)]
    averaged = [[None] * cols for _ in range(2)]
    for col in range(cols):
        total = total_ref[col]
        inverse = 1.0 / spread(total)
        offsets = (spread(moment_ref[col]) * inverse, spread(total * lag) * inverse)
        edges = (spread(edge_ref[col]) * inverse, spread(jnp.where(nyquist_lane, total, 0.0)) * inverse)
        lower = row_ref[col, 4] * (section > 0).astype(f32)
        upper = row_ref[col, 5] * (section < sec_total - 1).astype(f32)
        for dim in range(2):
            reverse = previous_section(-(offsets[dim] + float(PATCH) * edges[dim]))
            mean = (lower * reverse + upper * offsets[dim]) / jnp.maximum(lower + upper, 1.0)
            averaged[dim][col] = mean
            updated[dim][col] = field[dim][col] + step_size * mean
    flat = [updated[dim][col] for dim in range(2) for col in range(cols)]
    flat += [averaged[dim][col] for dim in range(2) for col in range(cols)]
    out_ref[...] = pack_columns(flat)


def final_kernel(cols, n_vertical, *refs):
    own, beside = refs[0][...], refs[1][...]
    vertical = unpack(refs[2][...], cols)
    vertical_beside = unpack(refs[3][...], cols)
    for k in range(1, n_vertical):
        vertical = add(vertical, unpack(refs[2 + 2 * k][...], cols))
        vertical_beside = add(vertical_beside, unpack(refs[3 + 2 * k][...], cols))
    field_ref, mean_ref = refs[2 + 2 * n_vertical :]
    core = lax.rem(lax.axis_index("sec"), 2)
    mine, other = unpack(own, cols), unpack(beside, cols)
    half = half_of()
    here = smoothed(mine, vertical, other, half, cols)
    there = smoothed(other, vertical_beside, mine, 1 - half, cols)
    mean_here, mean_there = unpack(own, cols, 2 * cols), unpack(beside, cols, 2 * cols)
    lane = lanes((1, PATCH))

    def pick(values):
        return jnp.where(core == 0, values[HALO : HALO + 1], values[HALO + 1 : HALO + 2])

    for out, a, b in ((field_ref, here, there), (mean_ref, mean_here, mean_there)):
        for dim in range(2):
            row = jnp.zeros((1, PATCH), f32)
            for col in range(cols):
                first = pick(jnp.where(half == 0, a[dim][col], b[dim][col]))
                second = pick(jnp.where(half == 0, b[dim][col], a[dim][col]))
                row = jnp.where(lane == col, first, row)
                row = jnp.where(lane == cols + col, second, row)
            out[dim, 0] = row[:, : 2 * cols]


def limit(mebibytes):
    return pltpu.CompilerParams(vmem_limit_bytes=mebibytes << 20)


def anywhere():
    return pl.BlockSpec(memory_space=pl.ANY)


def vmem():
    return pl.BlockSpec(memory_space=pltpu.VMEM)


def swap(pairs):
    return [(a, b) for a, b in pairs] + [(b, a) for a, b in pairs]


def per_device(section_images, displacement, fold_mask):
    n_sec, n_row = lax.axis_size("sec"), lax.axis_size("row")
    patch_cols = displacement.shape[-1]
    assert patch_cols % 2 == 0 and n_sec % 2 == 0
    assert section_images.shape[:2] == (1, PATCH)
    cols = patch_cols // 2
    chips = n_sec // 2
    spectrum_tables, shift_tables = [jnp.asarray(table) for table in tables()]

    def sections(pairs):
        return [(2 * a + c, 2 * b + c) for a, b in pairs for c in range(2)]

    swap_a = sections(swap([(j, j + 1) for j in range(0, chips - 1, 2)]))
    swap_b = sections(swap([(j, j + 1) for j in range(1, chips - 1, 2)]))
    far = swap([(2 * j + 1, 2 * j + 4) for j in range(chips - 2)])
    cores = swap([(2 * j, 2 * j + 1) for j in range(chips)])

    def between_cores(x):
        return lax.ppermute(x, "sec", cores)

    payload = pl.pallas_call(
        pack_kernel,
        out_shape=jax.ShapeDtypeStruct((PATCH + EXTRA, patch_cols * PATCH), bf16),
        in_specs=[anywhere()] * 3,
        out_specs=vmem(),
        scratch_shapes=[
            pltpu.SMEM(displacement.shape, f32),
            pltpu.SMEM(fold_mask.shape, jnp.int32),
            pltpu.SemaphoreType.DMA((3,)),
        ],
        compiler_params=limit(4),
        name="pack",
    )(*[pltpu.with_memory_space_constraint(x, pltpu.HBM) for x in (displacement, fold_mask, section_images)])
    received = [payload]
    for perm in (swap_a, swap_b, far):
        received.append(lax.ppermute(payload, "sec", perm))
    state = []
    for stage, block in enumerate(received):
        beside = between_cores(block)
        state = pl.pallas_call(
            lambda *refs, stage=stage: spectra_kernel(cols, stage, *refs),
            out_shape=(
                jax.ShapeDtypeStruct((WINDOW, cols, PATCH, PATCH), f32),
                jax.ShapeDtypeStruct((WINDOW, cols, PATCH, PATCH), f32),
                jax.ShapeDtypeStruct((cols, 6, WINDOW, PATCH), f32),
                jax.ShapeDtypeStruct((cols, WINDOW - 1, PATCH, 2 * PATCH), bf16),
            ),
            in_specs=[vmem()] * (3 + len(state)),
            out_specs=[vmem()] * 4,
            input_output_aliases={3 + k: k for k in range(len(state))},
            compiler_params=limit(16),
            cost_estimate=pl.CostEstimate(flops=500000000, bytes_accessed=1000000, transcendentals=0),
            name="spectra",
        )(block, beside, spectrum_tables, *state)
    base, stats = state[3], state[2]

    row_perms = [swap([(r, r + 1) for r in range(0, n_row - 1, 2)])]
    if n_row > 2:
        row_perms.append(swap([(r, r + 1) for r in range(1, n_row - 1, 2)]))

    def diagonal(x, rows):
        pairs = [(s * n_row + a, t * n_row + b) for s, t in cores for a, b in rows]
        return lax.ppermute(x, ("sec", "row"), pairs)

    messages = []
    for step in range(ITERS):
        out = pl.pallas_call(
            lambda *refs, step=step: iteration_kernel(cols, step, WINDOW - 1 - step, step == 0, len(row_perms), *refs),
            out_shape=jax.ShapeDtypeStruct((WINDOW, PATCH), f32),
            in_specs=[vmem()] * (3 + len(messages)),
            out_specs=vmem(),
            scratch_shapes=[pltpu.VMEM((cols, WINDOW, PATCH), f32)] * 3,
            compiler_params=limit(8),
            name="iteration",
        )(base, stats, shift_tables, *messages)
        beside = between_cores(out)
        rows = [diagonal(out, perm) for perm in row_perms]
        messages = [out, beside] + rows
    straight = [lax.ppermute(out, "row", perm) for perm in row_perms]
    messages = messages[:2] + [message for pair in zip(rows, straight) for message in pair]
    shape = jax.ShapeDtypeStruct(displacement.shape, f32)
    return pl.pallas_call(
        lambda *refs: final_kernel(cols, len(row_perms), *refs),
        out_shape=(shape, shape),
        in_specs=[vmem()] * len(messages),
        out_specs=(vmem(), vmem()),
        compiler_params=limit(4),
        name="final",
    )(*messages)


def solution(mesh):
    in_specs = (P("sec", "row", None), P(None, "sec", "row", None), P(None, "sec", "row", None))
    out_specs = (P(None, "sec", "row", None), P(None, "sec", "row", None))
    return jax.shard_map(per_device, mesh=mesh, in_specs=in_specs, out_specs=out_specs, check_vma=False)
```

```python
import math

import jax
import jax.numpy as jnp
import numpy as np
from jax import lax
from jax.experimental import pallas as pl
from jax.experimental.pallas import tpu as pltpu
from jax.sharding import PartitionSpec as P

PATCH = 128
HALF = PATCH // 2
ITERS = 3
HALO = 3
WINDOW = 8
EXTRA = 16
GROUP = 7

step_size = 0.5
stiffness = 0.2
epsilon = 1e-06
sharpness = 0.5 * PATCH
bf16 = jnp.bfloat16
f32 = jnp.float32


def split_table(table):
    table = np.asarray(table, np.float32)
    high = table.astype(bf16)
    low = (table - high.astype(np.float32)).astype(bf16)
    return high, low


def tables():
    n = PATCH
    index = np.arange(n)
    angle = 2.0 * np.pi / n * ((index[:, None] * index[None, :]) % n)
    cosine, sine = np.cos(angle), np.sin(angle)
    sign = 1.0 - 2.0 * (index % 2)

    basis = np.zeros((n, n))
    basis[:, :HALF] = cosine[:, :HALF]
    basis[:, HALF] = sign
    basis[:, HALF + 1 :] = -sine[:, 1:HALF]

    back = np.zeros((n, n))
    back[0] = 1.0
    back[1:HALF] = 2.0 * cosine[1:HALF]
    back[HALF] = sign
    back[HALF + 1 :] = -2.0 * sine[1:HALF]
    back /= n * n

    def doubled(table):
        pair = np.concatenate(split_table(table), axis=1)
        return np.concatenate([pair, pair], axis=0)

    down = np.concatenate(split_table(np.concatenate([cosine, -sine], axis=0)), axis=1)
    up = np.concatenate(split_table(np.concatenate([cosine, -sine], axis=1)), axis=0)
    return np.stack([doubled(basis), down, up]), doubled(back)


def split(values):
    high = values.astype(bf16)
    low = (values - high.astype(f32)).astype(bf16)
    return high, low


def dot(left, right):
    return jnp.dot(left, right, preferred_element_type=f32)


def fold(wide):
    return wide[:, :PATCH] + wide[:, PATCH:]


def lanes(shape):
    return lax.broadcasted_iota(jnp.int32, shape, len(shape) - 1)


def alternating(shape, dim):
    return (1 - 2 * (lax.broadcasted_iota(jnp.int32, shape, dim) % 2)).astype(f32)


def half_of():
    return lax.rem(lax.axis_index("sec") + lax.axis_index("row"), 2)


def pack_kernel(shift_ref, mask_ref, image_ref, out_ref, shift, mask, sems):
    copies = [
        pltpu.make_async_copy(image_ref.at[0], out_ref.at[:PATCH], sems.at[0]),
        pltpu.make_async_copy(shift_ref, shift, sems.at[1]),
        pltpu.make_async_copy(mask_ref, mask, sems.at[2]),
    ]
    for copy in copies:
        copy.start()
    copies[1].wait()
    copies[2].wait()
    row = lax.broadcasted_iota(jnp.int32, (EXTRA, PATCH), 0)
    for col in range(shift_ref.shape[-1]):
        values = jnp.zeros((EXTRA, PATCH), f32)
        for dim in range(2):
            value = jnp.full((EXTRA, PATCH), shift[dim, 0, 0, col], f32)
            high = value.astype(bf16).astype(f32)
            middle = (value - high).astype(bf16).astype(f32)
            low = (value - high) - middle
            allowed = jnp.full((EXTRA, PATCH), mask[dim, 0, 0, col].astype(f32), f32)
            for at, part in enumerate((high, middle, low)):
                values = jnp.where(row == 3 * dim + at, part, values)
            values = jnp.where(row == 6 + dim, allowed, values)
        out_ref[PATCH:, col * PATCH : (col + 1) * PATCH] = values.astype(bf16)
    copies[0].wait()


def forward_patches(patches, basis, down):
    count = len(patches)
    values = [patch.astype(f32) for patch in patches]
    totals = [jnp.sum(jnp.sum(value, axis=0, keepdims=True), axis=1, keepdims=True) for value in values]
    values = [value - total * (1.0 / (PATCH * PATCH)) for value, total in zip(values, totals)]
    left = jnp.concatenate([jnp.concatenate(split(value), axis=1) for value in values], axis=0)
    rows = fold(dot(left, basis))
    rows = [rows[k * PATCH : (k + 1) * PATCH] for k in range(count)]
    pairs = [jnp.concatenate(split(row), axis=1) for row in rows]
    both = [fold(dot(down, jnp.concatenate([pair, pair], axis=0))) for pair in pairs]
    lane = lanes((1, PATCH))
    sigma = jnp.where(lane > HALF, 1.0, -1.0) * jnp.where(lane % HALF == 0, 0.0, 1.0)
    sign = alternating((PATCH, PATCH), 0)
    result = []
    for row, wide in zip(rows, both):
        first, second = wide[:PATCH], wide[PATCH:]
        real = first + sigma * pltpu.roll(second, HALF, 1)
        imag = second - sigma * pltpu.roll(first, HALF, 1)
        energy_row = jnp.sum(row * row, axis=0, keepdims=True)
        nyquist_row = jnp.sum(row * sign, axis=0, keepdims=True)
        result.append((real, imag, energy_row, nyquist_row))
    return result


def slot_of(name):
    sec = lax.axis_index("sec")
    core = lax.rem(sec, 2)
    odd = lax.rem(sec // 2, 2)
    source, swapped = name
    if swapped:
        core = 1 - core
    if source == "own":
        return HALO + core
    if source == "a":
        return 5 - 4 * odd + core
    if source == "b":
        return 1 + 4 * odd + core
    return (WINDOW - 1) * core


def spectra_kernel(cols, names, pairs, starts, *refs):
    blocks, tables_ref = refs[: len(names)], refs[len(names)]
    basis_ref, down_ref, up_ref = [tables_ref.at[k] for k in range(3)]
    real_ref, imag_ref, row_ref, base_ref = refs[-4:]
    if starts:
        row_ref[...] = jnp.zeros(row_ref.shape, f32)
    half = half_of()
    slots = [slot_of(name) for name in names]
    places = [(block, slot, col) for block, slot in zip(blocks, slots) for col in range(cols)]
    starts = [pl.multiple_of((half * cols + col) * PATCH, PATCH) for col in range(cols)]
    patches = [block[:PATCH, pl.ds(starts[col], PATCH)] for block, slot, col in places]
    results = forward_patches(patches, basis_ref[...], down_ref[...])
    for (block, slot, col), (real, imag, energy_row, nyquist_row) in zip(places, results):
        real_ref[slot, col] = real
        imag_ref[slot, col] = imag
        row_ref[col, 0, pl.ds(slot, 1), :] = energy_row
        row_ref[col, 1, pl.ds(slot, 1), :] = nyquist_row
        small = block[PATCH:, pl.ds(starts[col], PATCH)].astype(f32)
        for dim in range(2):
            shift = small[3 * dim : 3 * dim + 1] + small[3 * dim + 1 : 3 * dim + 2] + small[3 * dim + 2 : 3 * dim + 3]
            row_ref[col, 2 + dim, pl.ds(slot, 1), :] = shift
            row_ref[col, 4 + dim, pl.ds(slot, 1), :] = small[6 + dim : 7 + dim]
    low_lane = lanes((1, PATCH)) <= HALF
    products = []
    for pair in pairs:
        for col in range(cols):
            sr, si = real_ref[pair, col], imag_ref[pair, col]
            nr, ni = real_ref[pair + 1, col], imag_ref[pair + 1, col]
            same = sr * nr + si * ni
            cross = si * nr - sr * ni
            top = jnp.concatenate(split(jnp.where(low_lane, same, cross)), axis=1)
            bottom = jnp.concatenate(split(jnp.where(low_lane, cross, -same)), axis=1)
            products.append(jnp.concatenate([top, bottom], axis=0))
    wides = [fold(dot(up_ref[...], product)) for product in products]
    bases = [jnp.concatenate(split(wide[:PATCH] + wide[PATCH:]), axis=1) for wide in wides]
    for k, base in enumerate(bases):
        base_ref[k % cols, pairs[k // cols]] = base


def energies(row_ref, col):
    lane = lanes((WINDOW, PATCH))
    weight = jnp.where(lane % HALF == 0, 1.0, 2.0)
    at_nyquist = jnp.where(lane == HALF, 1.0, 0.0)
    area = float(PATCH * PATCH)

    def spread(values):
        return jnp.broadcast_to(jnp.sum(values, axis=1, keepdims=True), (WINDOW, PATCH))

    energy, nyquist = row_ref[col, 0], row_ref[col, 1]
    corner = spread(nyquist * at_nyquist)
    corner_energy = corner * corner / area
    row_energy = spread(weight * (1.0 - at_nyquist) * nyquist * nyquist) / area
    col_energy = jnp.maximum(spread(energy * at_nyquist) / PATCH - corner_energy, 0.0)
    whole = spread(weight * energy) / PATCH
    bulk = jnp.maximum(whole - row_energy - col_energy - corner_energy, 0.0)
    return bulk, row_energy, col_energy, corner_energy, corner


def sine_cosine(z):
    zz = z * z
    sine = jnp.full_like(z, 1.0 / 6227020800.0)
    for factor in (-1.0 / 39916800.0, 1.0 / 362880.0, -1.0 / 5040.0, 1.0 / 120.0, -1.0 / 6.0, 1.0):
        sine = sine * zz + factor
    cosine = jnp.full_like(z, 1.0 / 479001600.0)
    for factor in (-1.0 / 3628800.0, 1.0 / 40320.0, -1.0 / 720.0, 1.0 / 24.0, -0.5, 1.0):
        cosine = cosine * zz + factor
    return sine * z, cosine


def cos_sin_turns(turns):
    sine, cosine = sine_cosine((turns - jnp.round(turns)) * math.pi)
    return 1.0 - 2.0 * sine * sine, 2.0 * sine * cosine


def shift_row(delta, gamma, lane):
    whole = jnp.round(delta)
    rest = delta - whole
    lag = lane.astype(f32) + whole
    lag = lag - PATCH * jnp.round(lag * (1.0 / PATCH))
    parity = (1 - 2 * (lag.astype(jnp.int32) & 1)).astype(f32)
    top, bottom = sine_cosine(rest * math.pi)
    sine, cosine = sine_cosine((lag + rest) * (math.pi / PATCH))
    centre = sine == 0.0
    ratio = jnp.where(centre, float(PATCH), top) / jnp.where(centre, 1.0, sine)
    nyquist = (1 - 2 * (lane & 1)).astype(f32) * gamma
    return (parity * (ratio * cosine - bottom) + nyquist) * (1.0 / PATCH)


def next_section(values):
    return pltpu.roll(values, WINDOW - 1, 0)


def previous_section(values):
    return pltpu.roll(values, 1, 0)


def column(message, lane):
    return jnp.broadcast_to(message[:, lane : lane + 1], (WINDOW, PATCH))


def pack_columns(values):
    lane = lanes((WINDOW, PATCH))
    packed = jnp.zeros((WINDOW, PATCH), f32)
    for at, value in enumerate(values):
        packed = jnp.where(lane == at, value, packed)
    return packed


def smoothed(updated, vertical, beside, half, cols):
    result = []
    for dim in range(2):
        current = []
        for col in range(cols):
            if col > 0:
                left = updated[dim][col - 1]
            else:
                left = jnp.where(half == 1, beside[dim][cols - 1], 0.0)
            if col < cols - 1:
                right = updated[dim][col + 1]
            else:
                right = jnp.where(half == 0, beside[dim][0], 0.0)
            own = updated[dim][col]
            current.append(own + stiffness * (left + right + vertical[dim][col] - 4.0 * own))
        result.append(current)
    return result


def unpack(message, cols, start=0):
    return [[column(message, start + dim * cols + col) for col in range(cols)] for dim in range(2)]


def add(left, right):
    return [[a + b for a, b in zip(x, y)] for x, y in zip(left, right)]


def iteration_kernel(cols, first, last, starts, n_vertical, *refs):
    base_ref, row_ref, back_ref = refs[:3]
    refs = refs[3:]
    core = lax.rem(lax.axis_index("sec"), 2)
    half = half_of()
    if starts:
        field = [[row_ref[col, 2 + dim] for col in range(cols)] for dim in range(2)]
    else:
        own_message, beside_message = refs[:2]
        vertical = unpack(refs[2][...], cols)
        for extra in refs[3 : 2 + n_vertical]:
            vertical = add(vertical, unpack(extra[...], cols))
        refs = refs[2 + n_vertical :]
        field = smoothed(unpack(own_message[...], cols), vertical, unpack(beside_message[...], cols), half, cols)
    out_ref, total_ref, moment_ref, edge_ref = refs
    lane = lanes((WINDOW, PATCH))
    frequency = (lane % HALF).astype(f32) * (1.0 / PATCH)
    high_lane = lane >= HALF
    nyquist_lane = lane == HALF
    zero_lane = lane % HALF == 0
    rows, turn_cos, turn_sin, ripple = [], [], [], []
    for col in range(cols):
        dy, dx = field[0][col], field[1][col]
        cos_y, sin_y = cos_sin_turns(dy * 0.5)
        cos_x, sin_x = cos_sin_turns(dx * 0.5)
        cos_both = cos_y * cos_x - sin_y * sin_x
        bulk, row_energy, col_energy, corner_energy, nyquist = energies(row_ref, col)
        energy = bulk + cos_y * cos_y * row_energy + cos_x * cos_x * col_energy + cos_both * cos_both * corner_energy
        scale = (sharpness / math.log(2.0)) / jnp.sqrt(energy * next_section(energy) + epsilon)
        gamma_y = cos_y * next_section(cos_y)
        gamma_x = cos_x * next_section(cos_x)
        gamma = cos_both * next_section(cos_both)
        corner = nyquist * next_section(nyquist) * (1.0 / (PATCH * PATCH))
        ripple.append((gamma - gamma_y * gamma_x) * corner * scale)
        rows.append(shift_row(dy - next_section(dy), gamma_y, lane))
        cosine, sine = cos_sin_turns((dx - next_section(dx)) * frequency)
        turn_cos.append(jnp.where(nyquist_lane, gamma_x, cosine) * scale)
        turn_sin.append(jnp.where(zero_lane, 0.0, jnp.where(high_lane, -sine, sine)) * scale)
    checker = alternating((WINDOW, PATCH), 0) * alternating((WINDOW, PATCH), 1)
    blocks = PATCH // WINDOW
    block_lag = [WINDOW * k - (PATCH if k >= blocks // 2 else 0) for k in range(blocks)]
    row_in_block = lax.broadcasted_iota(jnp.int32, (WINDOW, PATCH), 0).astype(f32)
    for col in range(cols):
        total_ref[col] = jnp.ones((WINDOW, PATCH), f32)
        moment_ref[col] = jnp.zeros((WINDOW, PATCH), f32)
        edge_ref[col] = jnp.zeros((WINDOW, PATCH), f32)
    tasks = [(pair, col) for pair in range(first, last) for col in range(cols)]
    size = -(-len(tasks) // -(-len(tasks) // GROUP))
    for at in range(0, len(tasks), size):
        group = tasks[at : at + size]
        moved = []
        for pair, col in group:
            row = slice(pair, pair + 1)
            shifter = pltpu.roll(jnp.broadcast_to(rows[col][row], (PATCH, PATCH)), 0, 1, stride=1, stride_axis=0)
            base = base_ref[col, pair]
            moved.append(fold(dot(jnp.concatenate(split(shifter), axis=1), jnp.concatenate([base, base], axis=0))))
        turned = []
        for (pair, col), value in zip(group, moved):
            row = slice(pair, pair + 1)
            value = value * turn_cos[col][row] + pltpu.roll(value, HALF, 1) * turn_sin[col][row]
            turned.append(jnp.concatenate(split(value), axis=1))
        wide = fold(dot(jnp.concatenate(turned, axis=0), back_ref[...]))
        for k, (pair, col) in enumerate(group):
            row = slice(pair, pair + 1)
            scores = wide[k * PATCH : (k + 1) * PATCH].reshape(blocks, WINDOW, PATCH)
            weights = jnp.exp2(scores + (ripple[col][row] * checker)[None])
            total = weights[0]
            moment = weights[0] * float(block_lag[0])
            for m in range(1, blocks):
                total = total + weights[m]
                moment = moment + weights[m] * float(block_lag[m])
            moment = moment + row_in_block * total
            total_ref[col, row, :] = jnp.sum(total, axis=0, keepdims=True)
            moment_ref[col, row, :] = jnp.sum(moment, axis=0, keepdims=True)
            edge_ref[col, row, :] = weights[blocks // 2, 0:1]
    sec_total = lax.axis_size("sec")
    section = lax.broadcasted_iota(jnp.int32, (WINDOW, PATCH), 0) + (lax.axis_index("sec") - core - HALO)
    lag = jnp.where(high_lane, lane - PATCH, lane).astype(f32)

    def spread(values):
        return jnp.broadcast_to(jnp.sum(values, axis=1, keepdims=True), (WINDOW, PATCH))

    updated = [[None] * cols for _ in range(2)]
    averaged = [[None] * cols for _ in range(2)]
    for col in range(cols):
        total = total_ref[col]
        inverse = 1.0 / spread(total)
        offsets = (spread(moment_ref[col]) * inverse, spread(total * lag) * inverse)
        edges = (spread(edge_ref[col]) * inverse, spread(jnp.where(nyquist_lane, total, 0.0)) * inverse)
        lower = row_ref[col, 4] * (section > 0).astype(f32)
        upper = row_ref[col, 5] * (section < sec_total - 1).astype(f32)
        for dim in range(2):
            reverse = previous_section(-(offsets[dim] + float(PATCH) * edges[dim]))
            mean = (lower * reverse + upper * offsets[dim]) / jnp.maximum(lower + upper, 1.0)
            averaged[dim][col] = mean
            updated[dim][col] = field[dim][col] + step_size * mean
    flat = [updated[dim][col] for dim in range(2) for col in range(cols)]
    flat += [averaged[dim][col] for dim in range(2) for col in range(cols)]
    out_ref[...] = pack_columns(flat)


def final_kernel(cols, n_vertical, *refs):
    own, beside = refs[0][...], refs[1][...]
    vertical = unpack(refs[2][...], cols)
    vertical_beside = unpack(refs[3][...], cols)
    for k in range(1, n_vertical):
        vertical = add(vertical, unpack(refs[2 + 2 * k][...], cols))
        vertical_beside = add(vertical_beside, unpack(refs[3 + 2 * k][...], cols))
    field_ref, mean_ref = refs[2 + 2 * n_vertical :]
    core = lax.rem(lax.axis_index("sec"), 2)
    mine, other = unpack(own, cols), unpack(beside, cols)
    half = half_of()
    here = smoothed(mine, vertical, other, half, cols)
    there = smoothed(other, vertical_beside, mine, 1 - half, cols)
    mean_here, mean_there = unpack(own, cols, 2 * cols), unpack(beside, cols, 2 * cols)
    lane = lanes((1, PATCH))

    def pick(values):
        return jnp.where(core == 0, values[HALO : HALO + 1], values[HALO + 1 : HALO + 2])

    for out, a, b in ((field_ref, here, there), (mean_ref, mean_here, mean_there)):
        for dim in range(2):
            row = jnp.zeros((1, PATCH), f32)
            for col in range(cols):
                first = pick(jnp.where(half == 0, a[dim][col], b[dim][col]))
                second = pick(jnp.where(half == 0, b[dim][col], a[dim][col]))
                row = jnp.where(lane == col, first, row)
                row = jnp.where(lane == cols + col, second, row)
            out[dim, 0] = row[:, : 2 * cols]


def limit(mebibytes):
    return pltpu.CompilerParams(vmem_limit_bytes=mebibytes << 20)


def anywhere():
    return pl.BlockSpec(memory_space=pl.ANY)


def vmem():
    return pl.BlockSpec(memory_space=pltpu.VMEM)


def swap(pairs):
    return [(a, b) for a, b in pairs] + [(b, a) for a, b in pairs]


def per_device(section_images, displacement, fold_mask):
    n_sec, n_row = lax.axis_size("sec"), lax.axis_size("row")
    patch_cols = displacement.shape[-1]
    assert patch_cols % 2 == 0 and n_sec % 2 == 0
    assert section_images.shape[:2] == (1, PATCH)
    cols = patch_cols // 2
    chips = n_sec // 2
    spectrum_tables, back_table = [jnp.asarray(table) for table in tables()]

    def sections(pairs):
        return [(2 * a + c, 2 * b + c) for a, b in pairs for c in range(2)]

    swap_a = sections(swap([(j, j + 1) for j in range(0, chips - 1, 2)]))
    swap_b = sections(swap([(j, j + 1) for j in range(1, chips - 1, 2)]))
    far = swap([(2 * j + 1, 2 * j + 4) for j in range(chips - 2)])
    cores = swap([(2 * j, 2 * j + 1) for j in range(chips)])

    def between_cores(x):
        return lax.ppermute(x, "sec", cores)

    payload = pl.pallas_call(
        pack_kernel,
        out_shape=jax.ShapeDtypeStruct((PATCH + EXTRA, patch_cols * PATCH), bf16),
        in_specs=[anywhere()] * 3,
        out_specs=vmem(),
        scratch_shapes=[
            pltpu.SMEM(displacement.shape, f32),
            pltpu.SMEM(fold_mask.shape, jnp.int32),
            pltpu.SemaphoreType.DMA((3,)),
        ],
        compiler_params=limit(4),
        cost_estimate=pl.CostEstimate(flops=0, bytes_accessed=8000000, transcendentals=0),
        name="pack",
    )(*[pltpu.with_memory_space_constraint(x, pltpu.HBM) for x in (displacement, fold_mask, section_images)])
    blocks = {("own", 0): payload}
    for source, perm in (("a", swap_a), ("b", swap_b), ("far", far)):
        blocks[source, 0] = lax.ppermute(payload, "sec", perm)
    for source in ("own", "a", "b", "far"):
        blocks[source, 1] = between_cores(blocks[source, 0])
    state = []
    every = tuple(range(WINDOW - 1))
    for stage, (names, pairs) in enumerate(
        (
            ((("own", 0), ("own", 1)), (HALO,)),
            ((("a", 0),), ()),
            ((("b", 0), ("far", 0)), ()),
            ((("a", 1), ("b", 1), ("far", 1)), every[:HALO] + every[HALO + 1 :]),
        )
    ):
        state = pl.pallas_call(
            lambda *refs, names=names, pairs=pairs, stage=stage: spectra_kernel(cols, names, pairs, stage == 0, *refs),
            out_shape=(
                jax.ShapeDtypeStruct((WINDOW, cols, PATCH, PATCH), f32),
                jax.ShapeDtypeStruct((WINDOW, cols, PATCH, PATCH), f32),
                jax.ShapeDtypeStruct((cols, 6, WINDOW, PATCH), f32),
                jax.ShapeDtypeStruct((cols, WINDOW - 1, PATCH, 2 * PATCH), bf16),
            ),
            in_specs=[vmem()] * (len(names) + 1 + len(state)),
            out_specs=[vmem()] * 4,
            input_output_aliases={len(names) + 1 + k: k for k in range(len(state))},
            compiler_params=limit(16),
            cost_estimate=pl.CostEstimate(flops=500000000, bytes_accessed=1000000, transcendentals=0),
            name="spectra",
        )(*[blocks[name] for name in names], spectrum_tables, *state)
    base, stats = state[3], state[2]

    row_perms = [swap([(r, r + 1) for r in range(0, n_row - 1, 2)])]
    if n_row > 2:
        row_perms.append(swap([(r, r + 1) for r in range(1, n_row - 1, 2)]))

    def diagonal(x, rows):
        pairs = [(s * n_row + a, t * n_row + b) for s, t in cores for a, b in rows]
        return lax.ppermute(x, ("sec", "row"), pairs)

    messages = []
    for step in range(ITERS):
        out = pl.pallas_call(
            lambda *refs, step=step: iteration_kernel(cols, step, WINDOW - 1 - step, step == 0, len(row_perms), *refs),
            out_shape=jax.ShapeDtypeStruct((WINDOW, PATCH), f32),
            in_specs=[vmem()] * (3 + len(messages)),
            out_specs=vmem(),
            scratch_shapes=[pltpu.VMEM((cols, WINDOW, PATCH), f32)] * 3,
            compiler_params=limit(8),
            name="iteration",
        )(base, stats, back_table, *messages)
        beside = between_cores(out)
        rows = [diagonal(out, perm) for perm in row_perms]
        messages = [out, beside] + rows
    straight = [lax.ppermute(out, "row", perm) for perm in row_perms]
    messages = messages[:2] + [message for pair in zip(rows, straight) for message in pair]
    shape = jax.ShapeDtypeStruct(displacement.shape, f32)
    return pl.pallas_call(
        lambda *refs: final_kernel(cols, len(row_perms), *refs),
        out_shape=(shape, shape),
        in_specs=[vmem()] * len(messages),
        out_specs=(vmem(), vmem()),
        compiler_params=limit(4),
        name="final",
    )(*messages)


def solution(mesh):
    in_specs = (P("sec", "row", None), P(None, "sec", "row", None), P(None, "sec", "row", None))
    out_specs = (P(None, "sec", "row", None), P(None, "sec", "row", None))
    return jax.shard_map(per_device, mesh=mesh, in_specs=in_specs, out_specs=out_specs, check_vma=False)
```

```python
import math

import jax
import jax.numpy as jnp
import numpy as np
from jax import lax
from jax.experimental import pallas as pl
from jax.experimental.pallas import tpu as pltpu
from jax.sharding import PartitionSpec as P

PATCH = 128
HALF = PATCH // 2
ITERS = 3
HALO = 3
WINDOW = 8
EXTRA = 16
GROUP = 7
DEPTH = 1

step_size = 0.5
stiffness = 0.2
epsilon = 1e-06
sharpness = 0.5 * PATCH
bf16 = jnp.bfloat16
f32 = jnp.float32


def split_table(table):
    table = np.asarray(table, np.float32)
    high = table.astype(bf16)
    low = (table - high.astype(np.float32)).astype(bf16)
    return high, low


def tables():
    n = PATCH
    index = np.arange(n)
    angle = 2.0 * np.pi / n * ((index[:, None] * index[None, :]) % n)
    cosine, sine = np.cos(angle), np.sin(angle)
    sign = 1.0 - 2.0 * (index % 2)

    basis = np.zeros((n, n))
    basis[:, :HALF] = cosine[:, :HALF]
    basis[:, HALF] = sign
    basis[:, HALF + 1 :] = -sine[:, 1:HALF]

    back = np.zeros((n, n))
    back[0] = 1.0
    back[1:HALF] = 2.0 * cosine[1:HALF]
    back[HALF] = sign
    back[HALF + 1 :] = -2.0 * sine[1:HALF]
    back /= n * n

    def doubled(table):
        pair = np.concatenate(split_table(table), axis=1)
        return np.concatenate([pair, pair], axis=0)

    down = np.concatenate(split_table(np.concatenate([cosine, -sine], axis=0)), axis=1)
    up = np.concatenate(split_table(np.concatenate([cosine, -sine], axis=1)), axis=0)
    return np.stack([doubled(basis), down, up]), doubled(back)


def split(values):
    high = values.astype(bf16)
    low = (values - high.astype(f32)).astype(bf16)
    return high, low


def dot(left, right):
    return jnp.dot(left, right, preferred_element_type=f32)


def fold(wide):
    return wide[:, :PATCH] + wide[:, PATCH:]


def lanes(shape):
    return lax.broadcasted_iota(jnp.int32, shape, len(shape) - 1)


def alternating(shape, dim):
    return (1 - 2 * (lax.broadcasted_iota(jnp.int32, shape, dim) % 2)).astype(f32)


def half_of():
    return lax.rem(lax.axis_index("sec") + lax.axis_index("row"), 2)


def pack_kernel(shift_ref, mask_ref, image_ref, out_ref, shift, mask, sems):
    copies = [
        pltpu.make_async_copy(image_ref.at[0], out_ref.at[:PATCH], sems.at[0]),
        pltpu.make_async_copy(shift_ref, shift, sems.at[1]),
        pltpu.make_async_copy(mask_ref, mask, sems.at[2]),
    ]
    for copy in copies:
        copy.start()
    copies[1].wait()
    copies[2].wait()
    row = lax.broadcasted_iota(jnp.int32, (EXTRA, PATCH), 0)
    for col in range(shift_ref.shape[-1]):
        values = jnp.zeros((EXTRA, PATCH), f32)
        for dim in range(2):
            value = jnp.full((EXTRA, PATCH), shift[dim, 0, 0, col], f32)
            high = value.astype(bf16).astype(f32)
            middle = (value - high).astype(bf16).astype(f32)
            low = (value - high) - middle
            allowed = jnp.full((EXTRA, PATCH), mask[dim, 0, 0, col].astype(f32), f32)
            for at, part in enumerate((high, middle, low)):
                values = jnp.where(row == 3 * dim + at, part, values)
            values = jnp.where(row == 6 + dim, allowed, values)
        out_ref[PATCH:, col * PATCH : (col + 1) * PATCH] = values.astype(bf16)
    copies[0].wait()


def forward_patches(patches, basis, down):
    count = len(patches)
    values = [patch.astype(f32) for patch in patches]
    totals = [jnp.sum(jnp.sum(value, axis=0, keepdims=True), axis=1, keepdims=True) for value in values]
    values = [value - total * (1.0 / (PATCH * PATCH)) for value, total in zip(values, totals)]
    left = jnp.concatenate([jnp.concatenate(split(value), axis=1) for value in values], axis=0)
    rows = fold(dot(left, basis))
    rows = [rows[k * PATCH : (k + 1) * PATCH] for k in range(count)]
    pairs = [jnp.concatenate(split(row), axis=1) for row in rows]
    both = [fold(dot(down, jnp.concatenate([pair, pair], axis=0))) for pair in pairs]
    lane = lanes((1, PATCH))
    sigma = jnp.where(lane > HALF, 1.0, -1.0) * jnp.where(lane % HALF == 0, 0.0, 1.0)
    sign = alternating((PATCH, PATCH), 0)
    result = []
    for row, wide in zip(rows, both):
        first, second = wide[:PATCH], wide[PATCH:]
        real = first + sigma * pltpu.roll(second, HALF, 1)
        imag = second - sigma * pltpu.roll(first, HALF, 1)
        energy_row = jnp.sum(row * row, axis=0, keepdims=True)
        nyquist_row = jnp.sum(row * sign, axis=0, keepdims=True)
        result.append((real, imag, energy_row, nyquist_row))
    return result


def slot_of(name):
    sec = lax.axis_index("sec")
    core = lax.rem(sec, 2)
    odd = lax.rem(sec // 2, 2)
    source, swapped = name
    if swapped:
        core = 1 - core
    if source == "own":
        return HALO + core
    if source == "a":
        return 5 - 4 * odd + core
    if source == "b":
        return 1 + 4 * odd + core
    return (WINDOW - 1) * core


def spectra_kernel(cols, names, pairs, starts, *refs):
    blocks, tables_ref = refs[: len(names)], refs[len(names)]
    basis_ref, down_ref, up_ref = [tables_ref.at[k] for k in range(3)]
    real_ref, imag_ref, row_ref, base_ref = refs[-4:]
    if starts:
        row_ref[...] = jnp.zeros(row_ref.shape, f32)
    half = half_of()
    slots = [slot_of(name) for name in names]
    places = [(block, slot, col) for block, slot in zip(blocks, slots) for col in range(cols)]
    starts = [pl.multiple_of((half * cols + col) * PATCH, PATCH) for col in range(cols)]
    patches = [block[:PATCH, pl.ds(starts[col], PATCH)] for block, slot, col in places]
    results = forward_patches(patches, basis_ref[...], down_ref[...])
    for (block, slot, col), (real, imag, energy_row, nyquist_row) in zip(places, results):
        real_ref[slot, col] = real
        imag_ref[slot, col] = imag
        row_ref[col, 0, pl.ds(slot, 1), :] = energy_row
        row_ref[col, 1, pl.ds(slot, 1), :] = nyquist_row
        small = block[PATCH:, pl.ds(starts[col], PATCH)].astype(f32)
        for dim in range(2):
            shift = small[3 * dim : 3 * dim + 1] + small[3 * dim + 1 : 3 * dim + 2] + small[3 * dim + 2 : 3 * dim + 3]
            row_ref[col, 2 + dim, pl.ds(slot, 1), :] = shift
            row_ref[col, 4 + dim, pl.ds(slot, 1), :] = small[6 + dim : 7 + dim]
    low_lane = lanes((1, PATCH)) <= HALF
    products = []

    def finish(k):
        wide = fold(dot(up_ref[...], products[k]))
        base_ref[k % cols, pairs[k // cols]] = jnp.concatenate(split(wide[:PATCH] + wide[PATCH:]), axis=1)

    for pair in pairs:
        for col in range(cols):
            sr, si = real_ref[pair, col], imag_ref[pair, col]
            nr, ni = real_ref[pair + 1, col], imag_ref[pair + 1, col]
            same = sr * nr + si * ni
            cross = si * nr - sr * ni
            top = jnp.concatenate(split(jnp.where(low_lane, same, cross)), axis=1)
            bottom = jnp.concatenate(split(jnp.where(low_lane, cross, -same)), axis=1)
            products.append(jnp.concatenate([top, bottom], axis=0))
            if len(products) > DEPTH:
                finish(len(products) - 1 - DEPTH)
    for k in range(max(len(products) - DEPTH, 0), len(products)):
        finish(k)


def energies(row_ref, col):
    lane = lanes((WINDOW, PATCH))
    weight = jnp.where(lane % HALF == 0, 1.0, 2.0)
    at_nyquist = jnp.where(lane == HALF, 1.0, 0.0)
    area = float(PATCH * PATCH)

    def spread(values):
        return jnp.broadcast_to(jnp.sum(values, axis=1, keepdims=True), (WINDOW, PATCH))

    energy, nyquist = row_ref[col, 0], row_ref[col, 1]
    corner = spread(nyquist * at_nyquist)
    corner_energy = corner * corner / area
    row_energy = spread(weight * (1.0 - at_nyquist) * nyquist * nyquist) / area
    col_energy = jnp.maximum(spread(energy * at_nyquist) / PATCH - corner_energy, 0.0)
    whole = spread(weight * energy) / PATCH
    bulk = jnp.maximum(whole - row_energy - col_energy - corner_energy, 0.0)
    return bulk, row_energy, col_energy, corner_energy, corner


def sine_cosine(z):
    zz = z * z
    sine = jnp.full_like(z, 1.0 / 6227020800.0)
    for factor in (-1.0 / 39916800.0, 1.0 / 362880.0, -1.0 / 5040.0, 1.0 / 120.0, -1.0 / 6.0, 1.0):
        sine = sine * zz + factor
    cosine = jnp.full_like(z, 1.0 / 479001600.0)
    for factor in (-1.0 / 3628800.0, 1.0 / 40320.0, -1.0 / 720.0, 1.0 / 24.0, -0.5, 1.0):
        cosine = cosine * zz + factor
    return sine * z, cosine


def cos_sin_turns(turns):
    sine, cosine = sine_cosine((turns - jnp.round(turns)) * math.pi)
    return 1.0 - 2.0 * sine * sine, 2.0 * sine * cosine


def shift_row(delta, gamma, lane):
    whole = jnp.round(delta)
    rest = delta - whole
    lag = lane.astype(f32) + whole
    lag = lag - PATCH * jnp.round(lag * (1.0 / PATCH))
    parity = (1 - 2 * (lag.astype(jnp.int32) & 1)).astype(f32)
    top, bottom = sine_cosine(rest * math.pi)
    sine, cosine = sine_cosine((lag + rest) * (math.pi / PATCH))
    centre = sine == 0.0
    ratio = jnp.where(centre, float(PATCH), top) / jnp.where(centre, 1.0, sine)
    nyquist = (1 - 2 * (lane & 1)).astype(f32) * gamma
    return (parity * (ratio * cosine - bottom) + nyquist) * (1.0 / PATCH)


def next_section(values):
    return pltpu.roll(values, WINDOW - 1, 0)


def previous_section(values):
    return pltpu.roll(values, 1, 0)


def column(message, lane):
    return jnp.broadcast_to(message[:, lane : lane + 1], (WINDOW, PATCH))


def pack_columns(values):
    lane = lanes((WINDOW, PATCH))
    packed = jnp.zeros((WINDOW, PATCH), f32)
    for at, value in enumerate(values):
        packed = jnp.where(lane == at, value, packed)
    return packed


def smoothed(updated, vertical, beside, half, cols):
    result = []
    for dim in range(2):
        current = []
        for col in range(cols):
            if col > 0:
                left = updated[dim][col - 1]
            else:
                left = jnp.where(half == 1, beside[dim][cols - 1], 0.0)
            if col < cols - 1:
                right = updated[dim][col + 1]
            else:
                right = jnp.where(half == 0, beside[dim][0], 0.0)
            own = updated[dim][col]
            current.append(own + stiffness * (left + right + vertical[dim][col] - 4.0 * own))
        result.append(current)
    return result


def unpack(message, cols, start=0):
    return [[column(message, start + dim * cols + col) for col in range(cols)] for dim in range(2)]


def add(left, right):
    return [[a + b for a, b in zip(x, y)] for x, y in zip(left, right)]


def iteration_kernel(cols, first, last, starts, n_vertical, *refs):
    base_ref, row_ref, back_ref = refs[:3]
    refs = refs[3:]
    core = lax.rem(lax.axis_index("sec"), 2)
    half = half_of()
    if starts:
        field = [[row_ref[col, 2 + dim] for col in range(cols)] for dim in range(2)]
    else:
        own_message, beside_message = refs[:2]
        vertical = unpack(refs[2][...], cols)
        for extra in refs[3 : 2 + n_vertical]:
            vertical = add(vertical, unpack(extra[...], cols))
        refs = refs[2 + n_vertical :]
        field = smoothed(unpack(own_message[...], cols), vertical, unpack(beside_message[...], cols), half, cols)
    out_ref, total_ref, moment_ref, edge_ref = refs
    lane = lanes((WINDOW, PATCH))
    frequency = (lane % HALF).astype(f32) * (1.0 / PATCH)
    high_lane = lane >= HALF
    nyquist_lane = lane == HALF
    zero_lane = lane % HALF == 0
    rows, turn_cos, turn_sin, ripple = [], [], [], []
    for col in range(cols):
        dy, dx = field[0][col], field[1][col]
        cos_y, sin_y = cos_sin_turns(dy * 0.5)
        cos_x, sin_x = cos_sin_turns(dx * 0.5)
        cos_both = cos_y * cos_x - sin_y * sin_x
        bulk, row_energy, col_energy, corner_energy, nyquist = energies(row_ref, col)
        energy = bulk + cos_y * cos_y * row_energy + cos_x * cos_x * col_energy + cos_both * cos_both * corner_energy
        scale = (sharpness / math.log(2.0)) / jnp.sqrt(energy * next_section(energy) + epsilon)
        gamma_y = cos_y * next_section(cos_y)
        gamma_x = cos_x * next_section(cos_x)
        gamma = cos_both * next_section(cos_both)
        corner = nyquist * next_section(nyquist) * (1.0 / (PATCH * PATCH))
        ripple.append((gamma - gamma_y * gamma_x) * corner * scale)
        rows.append(shift_row(dy - next_section(dy), gamma_y, lane))
        cosine, sine = cos_sin_turns((dx - next_section(dx)) * frequency)
        turn_cos.append(jnp.where(nyquist_lane, gamma_x, cosine) * scale)
        turn_sin.append(jnp.where(zero_lane, 0.0, jnp.where(high_lane, -sine, sine)) * scale)
    checker = alternating((WINDOW, PATCH), 0) * alternating((WINDOW, PATCH), 1)
    blocks = PATCH // WINDOW
    block_lag = [WINDOW * k - (PATCH if k >= blocks // 2 else 0) for k in range(blocks)]
    row_in_block = lax.broadcasted_iota(jnp.int32, (WINDOW, PATCH), 0).astype(f32)
    for col in range(cols):
        total_ref[col] = jnp.ones((WINDOW, PATCH), f32)
        moment_ref[col] = jnp.zeros((WINDOW, PATCH), f32)
        edge_ref[col] = jnp.zeros((WINDOW, PATCH), f32)
    tasks = [(pair, col) for pair in range(first, last) for col in range(cols)]
    size = -(-len(tasks) // -(-len(tasks) // GROUP))
    for at in range(0, len(tasks), size):
        group = tasks[at : at + size]
        moved = []
        for pair, col in group:
            row = slice(pair, pair + 1)
            shifter = pltpu.roll(jnp.broadcast_to(rows[col][row], (PATCH, PATCH)), 0, 1, stride=1, stride_axis=0)
            base = base_ref[col, pair]
            moved.append(fold(dot(jnp.concatenate(split(shifter), axis=1), jnp.concatenate([base, base], axis=0))))
        turned = []
        for (pair, col), value in zip(group, moved):
            row = slice(pair, pair + 1)
            value = value * turn_cos[col][row] + pltpu.roll(value, HALF, 1) * turn_sin[col][row]
            turned.append(jnp.concatenate(split(value), axis=1))
        wide = fold(dot(jnp.concatenate(turned, axis=0), back_ref[...]))
        for k, (pair, col) in enumerate(group):
            row = slice(pair, pair + 1)
            scores = wide[k * PATCH : (k + 1) * PATCH].reshape(blocks, WINDOW, PATCH)
            weights = jnp.exp2(scores + (ripple[col][row] * checker)[None])
            total = weights[0]
            moment = weights[0] * float(block_lag[0])
            for m in range(1, blocks):
                total = total + weights[m]
                moment = moment + weights[m] * float(block_lag[m])
            moment = moment + row_in_block * total
            total_ref[col, row, :] = jnp.sum(total, axis=0, keepdims=True)
            moment_ref[col, row, :] = jnp.sum(moment, axis=0, keepdims=True)
            edge_ref[col, row, :] = weights[blocks // 2, 0:1]
    sec_total = lax.axis_size("sec")
    section = lax.broadcasted_iota(jnp.int32, (WINDOW, PATCH), 0) + (lax.axis_index("sec") - core - HALO)
    lag = jnp.where(high_lane, lane - PATCH, lane).astype(f32)

    def spread(values):
        return jnp.broadcast_to(jnp.sum(values, axis=1, keepdims=True), (WINDOW, PATCH))

    updated = [[None] * cols for _ in range(2)]
    averaged = [[None] * cols for _ in range(2)]
    for col in range(cols):
        total = total_ref[col]
        inverse = 1.0 / spread(total)
        offsets = (spread(moment_ref[col]) * inverse, spread(total * lag) * inverse)
        edges = (spread(edge_ref[col]) * inverse, spread(jnp.where(nyquist_lane, total, 0.0)) * inverse)
        lower = row_ref[col, 4] * (section > 0).astype(f32)
        upper = row_ref[col, 5] * (section < sec_total - 1).astype(f32)
        for dim in range(2):
            reverse = previous_section(-(offsets[dim] + float(PATCH) * edges[dim]))
            mean = (lower * reverse + upper * offsets[dim]) / jnp.maximum(lower + upper, 1.0)
            averaged[dim][col] = mean
            updated[dim][col] = field[dim][col] + step_size * mean
    flat = [updated[dim][col] for dim in range(2) for col in range(cols)]
    flat += [averaged[dim][col] for dim in range(2) for col in range(cols)]
    out_ref[...] = pack_columns(flat)


def final_kernel(cols, n_vertical, *refs):
    own, beside = refs[0][...], refs[1][...]
    vertical = unpack(refs[2][...], cols)
    vertical_beside = unpack(refs[3][...], cols)
    for k in range(1, n_vertical):
        vertical = add(vertical, unpack(refs[2 + 2 * k][...], cols))
        vertical_beside = add(vertical_beside, unpack(refs[3 + 2 * k][...], cols))
    field_ref, mean_ref = refs[2 + 2 * n_vertical :]
    core = lax.rem(lax.axis_index("sec"), 2)
    mine, other = unpack(own, cols), unpack(beside, cols)
    half = half_of()
    here = smoothed(mine, vertical, other, half, cols)
    there = smoothed(other, vertical_beside, mine, 1 - half, cols)
    mean_here, mean_there = unpack(own, cols, 2 * cols), unpack(beside, cols, 2 * cols)
    lane = lanes((1, PATCH))

    def pick(values):
        return jnp.where(core == 0, values[HALO : HALO + 1], values[HALO + 1 : HALO + 2])

    for out, a, b in ((field_ref, here, there), (mean_ref, mean_here, mean_there)):
        for dim in range(2):
            row = jnp.zeros((1, PATCH), f32)
            for col in range(cols):
                first = pick(jnp.where(half == 0, a[dim][col], b[dim][col]))
                second = pick(jnp.where(half == 0, b[dim][col], a[dim][col]))
                row = jnp.where(lane == col, first, row)
                row = jnp.where(lane == cols + col, second, row)
            out[dim, 0] = row[:, : 2 * cols]


def limit(mebibytes):
    return pltpu.CompilerParams(vmem_limit_bytes=mebibytes << 20)


def anywhere():
    return pl.BlockSpec(memory_space=pl.ANY)


def vmem():
    return pl.BlockSpec(memory_space=pltpu.VMEM)


def swap(pairs):
    return [(a, b) for a, b in pairs] + [(b, a) for a, b in pairs]


def per_device(section_images, displacement, fold_mask):
    n_sec, n_row = lax.axis_size("sec"), lax.axis_size("row")
    patch_cols = displacement.shape[-1]
    assert patch_cols % 2 == 0 and n_sec % 2 == 0
    assert section_images.shape[:2] == (1, PATCH)
    cols = patch_cols // 2
    chips = n_sec // 2
    spectrum_tables, back_table = [jnp.asarray(table) for table in tables()]

    def sections(pairs):
        return [(2 * a + c, 2 * b + c) for a, b in pairs for c in range(2)]

    swap_a = sections(swap([(j, j + 1) for j in range(0, chips - 1, 2)]))
    swap_b = sections(swap([(j, j + 1) for j in range(1, chips - 1, 2)]))
    far = swap([(2 * j + 1, 2 * j + 4) for j in range(chips - 2)])
    cores = swap([(2 * j, 2 * j + 1) for j in range(chips)])

    def between_cores(x):
        return lax.ppermute(x, "sec", cores)

    payload = pl.pallas_call(
        pack_kernel,
        out_shape=jax.ShapeDtypeStruct((PATCH + EXTRA, patch_cols * PATCH), bf16),
        in_specs=[anywhere()] * 3,
        out_specs=vmem(),
        scratch_shapes=[
            pltpu.SMEM(displacement.shape, f32),
            pltpu.SMEM(fold_mask.shape, jnp.int32),
            pltpu.SemaphoreType.DMA((3,)),
        ],
        compiler_params=limit(4),
        cost_estimate=pl.CostEstimate(flops=0, bytes_accessed=8000000, transcendentals=0),
        name="pack",
    )(*[pltpu.with_memory_space_constraint(x, pltpu.HBM) for x in (displacement, fold_mask, section_images)])
    blocks = {("own", 0): payload}
    for source, perm in (("a", swap_a), ("b", swap_b), ("far", far)):
        blocks[source, 0] = lax.ppermute(payload, "sec", perm)
    for source in ("own", "a", "b", "far"):
        blocks[source, 1] = between_cores(blocks[source, 0])
    state = []
    row_perms = [swap([(r, r + 1) for r in range(0, n_row - 1, 2)])]
    if n_row > 2:
        row_perms.append(swap([(r, r + 1) for r in range(1, n_row - 1, 2)]))
    every = tuple(range(WINDOW - 1))
    stages = (
        ((("own", 0), ("own", 1)), (HALO,)),
        ((("a", 0),), ()),
        ((("b", 0), ("far", 0)), ()),
        ((("a", 1), ("b", 1), ("far", 1)), every[:HALO] + every[HALO + 1 :]),
    )
    state_shapes = [
        jax.ShapeDtypeStruct((WINDOW, cols, PATCH, PATCH), f32),
        jax.ShapeDtypeStruct((WINDOW, cols, PATCH, PATCH), f32),
        jax.ShapeDtypeStruct((cols, 6, WINDOW, PATCH), f32),
        jax.ShapeDtypeStruct((cols, WINDOW - 1, PATCH, 2 * PATCH), bf16),
    ]
    message_shape = jax.ShapeDtypeStruct((WINDOW, PATCH), f32)
    sums = [pltpu.VMEM((cols, WINDOW, PATCH), f32)] * 3
    for stage, (names, pairs) in enumerate(stages):
        last = stage == len(stages) - 1
        operands = [blocks[name] for name in names] + [spectrum_tables]

        def stage_kernel(*refs, names=names, pairs=pairs, stage=stage, last=last):
            if not last:
                spectra_kernel(cols, names, pairs, stage == 0, *refs)
                return
            count = len(names) + 1
            outs = refs[count + 5 :]
            spectra_kernel(cols, names, pairs, False, *refs[:count], *outs[:4])
            iteration_kernel(cols, 0, WINDOW - 1, True, 0, outs[3], outs[2], refs[count], *outs[4:])

        first_alias = len(operands) + last
        state = pl.pallas_call(
            stage_kernel,
            out_shape=state_shapes + [message_shape] * last,
            in_specs=[vmem()] * (first_alias + len(state)),
            out_specs=[vmem()] * (4 + last),
            scratch_shapes=sums * last,
            input_output_aliases={first_alias + k: k for k in range(len(state))},
            compiler_params=limit(16),
            cost_estimate=pl.CostEstimate(flops=500000000, bytes_accessed=1000000, transcendentals=0),
            name="spectra",
        )(*operands, *[back_table] * last, *state)
    base, stats, out = state[3], state[2], state[4]

    def diagonal(x, rows):
        pairs = [(s * n_row + a, t * n_row + b) for s, t in cores for a, b in rows]
        return lax.ppermute(x, ("sec", "row"), pairs)

    messages = []
    for step in range(ITERS):
        if step > 0:
            out = pl.pallas_call(
                lambda *refs, step=step: iteration_kernel(cols, step, WINDOW - 1 - step, False, len(row_perms), *refs),
                out_shape=message_shape,
                in_specs=[vmem()] * (3 + len(messages)),
                out_specs=vmem(),
                scratch_shapes=sums,
                compiler_params=limit(8),
                name="iteration",
            )(base, stats, back_table, *messages)
        beside = between_cores(out)
        rows = [diagonal(out, perm) for perm in row_perms]
        messages = [out, beside] + rows
    straight = [between_cores(message) for message in rows]
    messages = messages[:2] + [message for pair in zip(rows, straight) for message in pair]
    shape = jax.ShapeDtypeStruct(displacement.shape, f32)
    return pl.pallas_call(
        lambda *refs: final_kernel(cols, len(row_perms), *refs),
        out_shape=(shape, shape),
        in_specs=[vmem()] * len(messages),
        out_specs=(vmem(), vmem()),
        compiler_params=limit(4),
        name="final",
    )(*messages)


def solution(mesh):
    in_specs = (P("sec", "row", None), P(None, "sec", "row", None), P(None, "sec", "row", None))
    out_specs = (P(None, "sec", "row", None), P(None, "sec", "row", None))
    return jax.shard_map(per_device, mesh=mesh, in_specs=in_specs, out_specs=out_specs, check_vma=False)
```

```python
import math

import jax
import jax.numpy as jnp
import numpy as np
from jax import lax
from jax.experimental import pallas as pl
from jax.experimental.pallas import tpu as pltpu
from jax.sharding import PartitionSpec as P

PATCH = 128
HALF = PATCH // 2
ITERS = 3
HALO = 3
WINDOW = 8
EXTRA = 16
FIRST_GROUP = 4
GROUP = 10
DEPTH = 1

step_size = 0.5
stiffness = 0.2
epsilon = 1e-06
sharpness = 0.5 * PATCH
bf16 = jnp.bfloat16
f32 = jnp.float32


def split_table(table):
    table = np.asarray(table, np.float32)
    high = table.astype(bf16)
    low = (table - high.astype(np.float32)).astype(bf16)
    return high, low


def tables():
    n = PATCH
    index = np.arange(n)
    angle = 2.0 * np.pi / n * ((index[:, None] * index[None, :]) % n)
    cosine, sine = np.cos(angle), np.sin(angle)
    sign = 1.0 - 2.0 * (index % 2)

    basis = np.zeros((n, n))
    basis[:, :HALF] = cosine[:, :HALF]
    basis[:, HALF] = sign
    basis[:, HALF + 1 :] = -sine[:, 1:HALF]

    back = np.zeros((n, n))
    back[0] = 1.0
    back[1:HALF] = 2.0 * cosine[1:HALF]
    back[HALF] = sign
    back[HALF + 1 :] = -2.0 * sine[1:HALF]
    back /= n * n

    def doubled(table):
        pair = np.concatenate(split_table(table), axis=1)
        return np.concatenate([pair, pair], axis=0)

    down = np.concatenate(split_table(np.concatenate([cosine, -sine], axis=0)), axis=1)
    up = np.concatenate(split_table(np.concatenate([cosine, -sine], axis=1)), axis=0)
    return np.stack([doubled(basis), down, up]), doubled(back)


def split(values):
    high = values.astype(bf16)
    low = (values - high.astype(f32)).astype(bf16)
    return high, low


def dot(left, right):
    return jnp.dot(left, right, preferred_element_type=f32)


def fold(wide):
    return wide[:, :PATCH] + wide[:, PATCH:]


def lanes(shape):
    return lax.broadcasted_iota(jnp.int32, shape, len(shape) - 1)


def alternating(shape, dim):
    return (1 - 2 * (lax.broadcasted_iota(jnp.int32, shape, dim) % 2)).astype(f32)


def half_of():
    return lax.rem(lax.axis_index("sec") + lax.axis_index("row"), 2)


def pack_kernel(shift_ref, mask_ref, image_ref, out_ref, shift, mask, sems):
    copies = [
        pltpu.make_async_copy(image_ref.at[0], out_ref.at[:PATCH], sems.at[0]),
        pltpu.make_async_copy(shift_ref, shift, sems.at[1]),
        pltpu.make_async_copy(mask_ref, mask, sems.at[2]),
    ]
    for copy in copies:
        copy.start()
    copies[1].wait()
    copies[2].wait()
    row = lax.broadcasted_iota(jnp.int32, (EXTRA, PATCH), 0)
    for col in range(shift_ref.shape[-1]):
        values = jnp.zeros((EXTRA, PATCH), f32)
        for dim in range(2):
            value = jnp.full((EXTRA, PATCH), shift[dim, 0, 0, col], f32)
            high = value.astype(bf16).astype(f32)
            middle = (value - high).astype(bf16).astype(f32)
            low = (value - high) - middle
            allowed = jnp.full((EXTRA, PATCH), mask[dim, 0, 0, col].astype(f32), f32)
            for at, part in enumerate((high, middle, low)):
                values = jnp.where(row == 3 * dim + at, part, values)
            values = jnp.where(row == 6 + dim, allowed, values)
        out_ref[PATCH:, col * PATCH : (col + 1) * PATCH] = values.astype(bf16)
    copies[0].wait()


def forward_patches(patches, basis, down, mean_row):
    count = len(patches)
    rows = fold(dot(jnp.concatenate(patches, axis=0), basis))
    lane = lanes((1, PATCH))
    sign = alternating((WINDOW, PATCH), 0)
    sigma = jnp.where(lane > HALF, 1.0, -1.0) * jnp.where(lane % HALF == 0, 0.0, 1.0)
    centred, nyquist_rows, pairs = [], [], []
    for k in range(count):
        row = rows[k * PATCH : (k + 1) * PATCH]
        part = jnp.sum(row.reshape(PATCH // WINDOW, WINDOW, PATCH), axis=0)
        whole = jnp.sum(part, axis=0, keepdims=True)
        row = row - (whole[:, :1] * (1.0 / (PATCH * PATCH))) * mean_row
        nyquist_rows.append(jnp.sum(part * sign, axis=0, keepdims=True))
        pair = jnp.concatenate(split(row), axis=1)
        centred.append(row)
        pairs.append(jnp.concatenate([pair, pair], axis=0))
    both = [fold(dot(down, pair)) for pair in pairs]
    result = []
    for row, nyquist_row, wide in zip(centred, nyquist_rows, both):
        first, second = wide[:PATCH], wide[PATCH:]
        real = first + sigma * pltpu.roll(second, HALF, 1)
        imag = second - sigma * pltpu.roll(first, HALF, 1)
        result.append((real, imag, jnp.sum(row * row, axis=0, keepdims=True), nyquist_row))
    return result


def slot_of(name):
    sec = lax.axis_index("sec")
    core = lax.rem(sec, 2)
    odd = lax.rem(sec // 2, 2)
    source, swapped = name
    if swapped:
        core = 1 - core
    if source == "own":
        return HALO + core
    if source == "a":
        return 5 - 4 * odd + core
    if source == "b":
        return 1 + 4 * odd + core
    return (WINDOW - 1) * core


def spectra_kernel(cols, names, pairs, starts, *refs):
    blocks, tables_ref = refs[: len(names)], refs[len(names)]
    basis_ref, down_ref, up_ref = [tables_ref.at[k] for k in range(3)]
    basis = basis_ref[:PATCH]
    ones = jnp.sum(basis.astype(f32), axis=0, keepdims=True)
    mean_row = ones[:, :PATCH] + ones[:, PATCH:]
    real_ref, imag_ref, row_ref, base_ref = refs[-4:]
    if starts:
        row_ref[...] = jnp.zeros(row_ref.shape, f32)
    half = half_of()
    slots = [slot_of(name) for name in names]
    places = [(block, slot, col) for block, slot in zip(blocks, slots) for col in range(cols)]
    starts = [pl.multiple_of((half * cols + col) * PATCH, PATCH) for col in range(cols)]
    patches = [block[:PATCH, pl.ds(starts[col], PATCH)] for block, slot, col in places]
    results = forward_patches(patches, basis, down_ref[...], mean_row)
    for (block, slot, col), (real, imag, energy_row, nyquist_row) in zip(places, results):
        real_ref[slot, col] = real
        imag_ref[slot, col] = imag
        row_ref[col, 0, pl.ds(slot, 1), :] = energy_row
        row_ref[col, 1, pl.ds(slot, 1), :] = nyquist_row
        small = block[PATCH:, pl.ds(starts[col], PATCH)].astype(f32)
        for dim in range(2):
            shift = small[3 * dim : 3 * dim + 1] + small[3 * dim + 1 : 3 * dim + 2] + small[3 * dim + 2 : 3 * dim + 3]
            row_ref[col, 2 + dim, pl.ds(slot, 1), :] = shift
            row_ref[col, 4 + dim, pl.ds(slot, 1), :] = small[6 + dim : 7 + dim]
    low_lane = lanes((1, PATCH)) <= HALF
    products = []

    def finish(k):
        wide = fold(dot(up_ref[...], products[k]))
        base_ref[k % cols, pairs[k // cols]] = jnp.concatenate(split(wide[:PATCH] + wide[PATCH:]), axis=1)

    for pair in pairs:
        for col in range(cols):
            sr, si = real_ref[pair, col], imag_ref[pair, col]
            nr, ni = real_ref[pair + 1, col], imag_ref[pair + 1, col]
            same = sr * nr + si * ni
            cross = si * nr - sr * ni
            top = jnp.concatenate(split(jnp.where(low_lane, same, cross)), axis=1)
            bottom = jnp.concatenate(split(jnp.where(low_lane, cross, -same)), axis=1)
            products.append(jnp.concatenate([top, bottom], axis=0))
            if len(products) > DEPTH:
                finish(len(products) - 1 - DEPTH)
    for k in range(max(len(products) - DEPTH, 0), len(products)):
        finish(k)


def energies(row_ref, col):
    lane = lanes((WINDOW, PATCH))
    weight = jnp.where(lane % HALF == 0, 1.0, 2.0)
    at_nyquist = jnp.where(lane == HALF, 1.0, 0.0)
    area = float(PATCH * PATCH)

    def spread(values):
        return jnp.broadcast_to(jnp.sum(values, axis=1, keepdims=True), (WINDOW, PATCH))

    energy, nyquist = row_ref[col, 0], row_ref[col, 1]
    corner = spread(nyquist * at_nyquist)
    corner_energy = corner * corner / area
    row_energy = spread(weight * (1.0 - at_nyquist) * nyquist * nyquist) / area
    col_energy = jnp.maximum(spread(energy * at_nyquist) / PATCH - corner_energy, 0.0)
    whole = spread(weight * energy) / PATCH
    bulk = jnp.maximum(whole - row_energy - col_energy - corner_energy, 0.0)
    return bulk, row_energy, col_energy, corner_energy, corner


def sine_cosine(z):
    zz = z * z
    sine = jnp.full_like(z, 1.0 / 6227020800.0)
    for factor in (-1.0 / 39916800.0, 1.0 / 362880.0, -1.0 / 5040.0, 1.0 / 120.0, -1.0 / 6.0, 1.0):
        sine = sine * zz + factor
    cosine = jnp.full_like(z, 1.0 / 479001600.0)
    for factor in (-1.0 / 3628800.0, 1.0 / 40320.0, -1.0 / 720.0, 1.0 / 24.0, -0.5, 1.0):
        cosine = cosine * zz + factor
    return sine * z, cosine


def cos_sin_turns(turns):
    sine, cosine = sine_cosine((turns - jnp.round(turns)) * math.pi)
    return 1.0 - 2.0 * sine * sine, 2.0 * sine * cosine


def shift_row(delta, gamma, lane):
    whole = jnp.round(delta)
    rest = delta - whole
    lag = lane.astype(f32) + whole
    lag = lag - PATCH * jnp.round(lag * (1.0 / PATCH))
    parity = (1 - 2 * (lag.astype(jnp.int32) & 1)).astype(f32)
    top, bottom = sine_cosine(rest * math.pi)
    sine, cosine = sine_cosine((lag + rest) * (math.pi / PATCH))
    centre = sine == 0.0
    ratio = jnp.where(centre, float(PATCH), top) / jnp.where(centre, 1.0, sine)
    nyquist = (1 - 2 * (lane & 1)).astype(f32) * gamma
    return (parity * (ratio * cosine - bottom) + nyquist) * (1.0 / PATCH)


def next_section(values):
    return pltpu.roll(values, WINDOW - 1, 0)


def previous_section(values):
    return pltpu.roll(values, 1, 0)


def column(message, lane):
    return jnp.broadcast_to(message[:, lane : lane + 1], (WINDOW, PATCH))


def pack_columns(values):
    lane = lanes((WINDOW, PATCH))
    packed = jnp.zeros((WINDOW, PATCH), f32)
    for at, value in enumerate(values):
        packed = jnp.where(lane == at, value, packed)
    return packed


def smoothed(updated, vertical, beside, half, cols):
    result = []
    for dim in range(2):
        current = []
        for col in range(cols):
            if col > 0:
                left = updated[dim][col - 1]
            else:
                left = jnp.where(half == 1, beside[dim][cols - 1], 0.0)
            if col < cols - 1:
                right = updated[dim][col + 1]
            else:
                right = jnp.where(half == 0, beside[dim][0], 0.0)
            own = updated[dim][col]
            current.append(own + stiffness * (left + right + vertical[dim][col] - 4.0 * own))
        result.append(current)
    return result


def unpack(message, cols, start=0):
    return [[column(message, start + dim * cols + col) for col in range(cols)] for dim in range(2)]


def add(left, right):
    return [[a + b for a, b in zip(x, y)] for x, y in zip(left, right)]


def iteration_kernel(cols, first, last, starts, n_vertical, *refs):
    base_ref, row_ref, back_ref = refs[:3]
    refs = refs[3:]
    core = lax.rem(lax.axis_index("sec"), 2)
    half = half_of()
    if starts:
        field = [[row_ref[col, 2 + dim] for col in range(cols)] for dim in range(2)]
    else:
        own_message, beside_message = refs[:2]
        vertical = unpack(refs[2][...], cols)
        for extra in refs[3 : 2 + n_vertical]:
            vertical = add(vertical, unpack(extra[...], cols))
        refs = refs[2 + n_vertical :]
        field = smoothed(unpack(own_message[...], cols), vertical, unpack(beside_message[...], cols), half, cols)
    out_ref, total_ref, moment_ref, edge_ref = refs
    lane = lanes((WINDOW, PATCH))
    frequency = (lane % HALF).astype(f32) * (1.0 / PATCH)
    high_lane = lane >= HALF
    nyquist_lane = lane == HALF
    zero_lane = lane % HALF == 0
    rows, turn_cos, turn_sin, ripple = [], [], [], []
    for col in range(cols):
        dy, dx = field[0][col], field[1][col]
        cos_y, sin_y = cos_sin_turns(dy * 0.5)
        cos_x, sin_x = cos_sin_turns(dx * 0.5)
        cos_both = cos_y * cos_x - sin_y * sin_x
        bulk, row_energy, col_energy, corner_energy, nyquist = [row_ref[col, 6 + k] for k in range(5)]
        energy = bulk + cos_y * cos_y * row_energy + cos_x * cos_x * col_energy + cos_both * cos_both * corner_energy
        scale = (sharpness / math.log(2.0)) / jnp.sqrt(energy * next_section(energy) + epsilon)
        gamma_y = cos_y * next_section(cos_y)
        gamma_x = cos_x * next_section(cos_x)
        gamma = cos_both * next_section(cos_both)
        corner = nyquist * next_section(nyquist) * (1.0 / (PATCH * PATCH))
        ripple.append((gamma - gamma_y * gamma_x) * corner * scale)
        rows.append(shift_row(dy - next_section(dy), gamma_y, lane))
        cosine, sine = cos_sin_turns((dx - next_section(dx)) * frequency)
        turn_cos.append(jnp.where(nyquist_lane, gamma_x, cosine) * scale)
        turn_sin.append(jnp.where(zero_lane, 0.0, jnp.where(high_lane, -sine, sine)) * scale)
    checker = alternating((WINDOW, PATCH), 0) * alternating((WINDOW, PATCH), 1)
    blocks = PATCH // WINDOW
    block_order = [(blocks // 2 - 1 - k) % blocks for k in range(blocks)]
    row_in_block = lax.broadcasted_iota(jnp.int32, (WINDOW, PATCH), 0).astype(f32)
    for col in range(cols):
        total_ref[col] = jnp.ones((WINDOW, PATCH), f32)
        moment_ref[col] = jnp.zeros((WINDOW, PATCH), f32)
        edge_ref[col] = jnp.zeros((WINDOW, PATCH), f32)
    tasks = [(pair, col) for pair in range(first, last) for col in range(cols)]
    most = FIRST_GROUP if starts else GROUP
    size = -(-len(tasks) // -(-len(tasks) // most))
    for at in range(0, len(tasks), size):
        group = tasks[at : at + size]
        moved = []
        for pair, col in group:
            row = slice(pair, pair + 1)
            parts = [part.astype(f32) for part in split(rows[col][row])]
            parts = [
                pltpu.roll(jnp.broadcast_to(part, (PATCH, PATCH)), 0, 1, stride=1, stride_axis=0).astype(bf16)
                for part in parts
            ]
            base = base_ref[col, pair]
            moved.append(fold(dot(jnp.concatenate(parts, axis=1), jnp.concatenate([base, base], axis=0))))
        turned = []
        for (pair, col), value in zip(group, moved):
            row = slice(pair, pair + 1)
            value = value * turn_cos[col][row] + pltpu.roll(value, HALF, 1) * turn_sin[col][row]
            turned.append(jnp.concatenate(split(value), axis=1))
        wide = fold(dot(jnp.concatenate(turned, axis=0), back_ref[...]))
        for k, (pair, col) in enumerate(group):
            row = slice(pair, pair + 1)
            scores = wide[k * PATCH : (k + 1) * PATCH].reshape(blocks, WINDOW, PATCH)
            weights = jnp.exp2(scores + (ripple[col][row] * checker)[None])
            total = weights[block_order[0]]
            moment = total
            for m in block_order[1:-1]:
                total = total + weights[m]
                moment = moment + total
            total = total + weights[block_order[-1]]
            moment = float(WINDOW) * moment + (row_in_block - PATCH // 2) * total
            total_ref[col, row, :] = jnp.sum(total, axis=0, keepdims=True)
            moment_ref[col, row, :] = jnp.sum(moment, axis=0, keepdims=True)
            edge_ref[col, row, :] = weights[blocks // 2, 0:1]
    sec_total = lax.axis_size("sec")
    section = lax.broadcasted_iota(jnp.int32, (WINDOW, PATCH), 0) + (lax.axis_index("sec") - core - HALO)
    lag = jnp.where(high_lane, lane - PATCH, lane).astype(f32)

    def spread(values):
        return jnp.broadcast_to(jnp.sum(values, axis=1, keepdims=True), (WINDOW, PATCH))

    updated = [[None] * cols for _ in range(2)]
    averaged = [[None] * cols for _ in range(2)]
    for col in range(cols):
        total = total_ref[col]
        inverse = 1.0 / spread(total)
        offsets = (spread(moment_ref[col]) * inverse, spread(total * lag) * inverse)
        edges = (spread(edge_ref[col]) * inverse, spread(jnp.where(nyquist_lane, total, 0.0)) * inverse)
        lower = row_ref[col, 4] * (section > 0).astype(f32)
        upper = row_ref[col, 5] * (section < sec_total - 1).astype(f32)
        for dim in range(2):
            reverse = previous_section(-(offsets[dim] + float(PATCH) * edges[dim]))
            mean = (lower * reverse + upper * offsets[dim]) / jnp.maximum(lower + upper, 1.0)
            averaged[dim][col] = mean
            updated[dim][col] = field[dim][col] + step_size * mean
    flat = [updated[dim][col] for dim in range(2) for col in range(cols)]
    flat += [averaged[dim][col] for dim in range(2) for col in range(cols)]
    out_ref[...] = pack_columns(flat)


def final_kernel(cols, n_vertical, *refs):
    own, beside = refs[0][...], refs[1][...]
    vertical = unpack(refs[2][...], cols)
    vertical_beside = unpack(refs[3][...], cols)
    for k in range(1, n_vertical):
        vertical = add(vertical, unpack(refs[2 + 2 * k][...], cols))
        vertical_beside = add(vertical_beside, unpack(refs[3 + 2 * k][...], cols))
    field_ref, mean_ref = refs[2 + 2 * n_vertical :]
    core = lax.rem(lax.axis_index("sec"), 2)
    mine, other = unpack(own, cols), unpack(beside, cols)
    half = half_of()
    here = smoothed(mine, vertical, other, half, cols)
    there = smoothed(other, vertical_beside, mine, 1 - half, cols)
    mean_here, mean_there = unpack(own, cols, 2 * cols), unpack(beside, cols, 2 * cols)
    lane = lanes((1, PATCH))

    def pick(values):
        return jnp.where(core == 0, values[HALO : HALO + 1], values[HALO + 1 : HALO + 2])

    for out, a, b in ((field_ref, here, there), (mean_ref, mean_here, mean_there)):
        for dim in range(2):
            row = jnp.zeros((1, PATCH), f32)
            for col in range(cols):
                first = pick(jnp.where(half == 0, a[dim][col], b[dim][col]))
                second = pick(jnp.where(half == 0, b[dim][col], a[dim][col]))
                row = jnp.where(lane == col, first, row)
                row = jnp.where(lane == cols + col, second, row)
            out[dim, 0] = row[:, : 2 * cols]


def limit(mebibytes):
    return pltpu.CompilerParams(vmem_limit_bytes=mebibytes << 20)


def anywhere():
    return pl.BlockSpec(memory_space=pl.ANY)


def vmem():
    return pl.BlockSpec(memory_space=pltpu.VMEM)


def swap(pairs):
    return [(a, b) for a, b in pairs] + [(b, a) for a, b in pairs]


def per_device(section_images, displacement, fold_mask):
    n_sec, n_row = lax.axis_size("sec"), lax.axis_size("row")
    patch_cols = displacement.shape[-1]
    assert patch_cols % 2 == 0 and n_sec % 2 == 0
    assert section_images.shape[:2] == (1, PATCH)
    cols = patch_cols // 2
    chips = n_sec // 2
    spectrum_tables, back_table = [jnp.asarray(table) for table in tables()]

    def sections(pairs):
        return [(2 * a + c, 2 * b + c) for a, b in pairs for c in range(2)]

    swap_a = sections(swap([(j, j + 1) for j in range(0, chips - 1, 2)]))
    swap_b = sections(swap([(j, j + 1) for j in range(1, chips - 1, 2)]))
    far = swap([(2 * j + 1, 2 * j + 4) for j in range(chips - 2)])
    cores = swap([(2 * j, 2 * j + 1) for j in range(chips)])

    def between_cores(x):
        return lax.ppermute(x, "sec", cores)

    payload = pl.pallas_call(
        pack_kernel,
        out_shape=jax.ShapeDtypeStruct((PATCH + EXTRA, patch_cols * PATCH), bf16),
        in_specs=[anywhere()] * 3,
        out_specs=vmem(),
        scratch_shapes=[
            pltpu.SMEM(displacement.shape, f32),
            pltpu.SMEM(fold_mask.shape, jnp.int32),
            pltpu.SemaphoreType.DMA((3,)),
        ],
        compiler_params=limit(4),
        cost_estimate=pl.CostEstimate(flops=0, bytes_accessed=8000000, transcendentals=0),
        name="pack",
    )(*[pltpu.with_memory_space_constraint(x, pltpu.HBM) for x in (displacement, fold_mask, section_images)])
    blocks = {("own", 0): payload}
    for source, perm in (("a", swap_a), ("b", swap_b), ("far", far)):
        blocks[source, 0] = lax.ppermute(payload, "sec", perm)
    for source in ("own", "a", "b", "far"):
        blocks[source, 1] = between_cores(blocks[source, 0])
    state = []
    row_perms = [swap([(r, r + 1) for r in range(0, n_row - 1, 2)])]
    if n_row > 2:
        row_perms.append(swap([(r, r + 1) for r in range(1, n_row - 1, 2)]))
    every = tuple(range(WINDOW - 1))
    stages = (
        ((("own", 0), ("own", 1)), (HALO,)),
        ((("a", 0),), ()),
        ((("a", 1), ("b", 0), ("far", 0)), ()),
        ((("b", 1), ("far", 1)), every[:HALO] + every[HALO + 1 :]),
    )
    state_shapes = [
        jax.ShapeDtypeStruct((WINDOW, cols, PATCH, PATCH), f32),
        jax.ShapeDtypeStruct((WINDOW, cols, PATCH, PATCH), f32),
        jax.ShapeDtypeStruct((cols, 11, WINDOW, PATCH), f32),
        jax.ShapeDtypeStruct((cols, WINDOW - 1, PATCH, 2 * PATCH), bf16),
    ]
    message_shape = jax.ShapeDtypeStruct((WINDOW, PATCH), f32)
    sums = [pltpu.VMEM((cols, WINDOW, PATCH), f32)] * 3
    for stage, (names, pairs) in enumerate(stages):
        last = stage == len(stages) - 1
        operands = [blocks[name] for name in names] + [spectrum_tables]

        def stage_kernel(*refs, names=names, pairs=pairs, stage=stage, last=last):
            if not last:
                spectra_kernel(cols, names, pairs, stage == 0, *refs)
                return
            count = len(names) + 1
            outs = refs[count + 5 :]
            spectra_kernel(cols, names, pairs, False, *refs[:count], *outs[:4])
            for col in range(cols):
                for k, value in enumerate(energies(outs[2], col)):
                    outs[2][col, 6 + k] = value
            iteration_kernel(cols, 0, WINDOW - 1, True, 0, outs[3], outs[2], refs[count], *outs[4:])

        first_alias = len(operands) + last
        state = pl.pallas_call(
            stage_kernel,
            out_shape=state_shapes + [message_shape] * last,
            in_specs=[vmem()] * (first_alias + len(state)),
            out_specs=[vmem()] * (4 + last),
            scratch_shapes=sums * last,
            input_output_aliases={first_alias + k: k for k in range(len(state))},
            compiler_params=limit(16),
            cost_estimate=pl.CostEstimate(flops=500000000, bytes_accessed=1000000, transcendentals=0),
            name="spectra",
        )(*operands, *[back_table] * last, *state)
    base, stats, out = state[3], state[2], state[4]

    def diagonal(x, rows):
        pairs = [(s * n_row + a, t * n_row + b) for s, t in cores for a, b in rows]
        return lax.ppermute(x, ("sec", "row"), pairs)

    messages = []
    for step in range(ITERS):
        if step > 0:
            out = pl.pallas_call(
                lambda *refs, step=step: iteration_kernel(cols, step, WINDOW - 1 - step, False, len(row_perms), *refs),
                out_shape=message_shape,
                in_specs=[vmem()] * (3 + len(messages)),
                out_specs=vmem(),
                scratch_shapes=sums,
                compiler_params=limit(8),
                name="iteration",
            )(base, stats, back_table, *messages)
        beside = between_cores(out)
        rows = [diagonal(out, perm) for perm in row_perms]
        messages = [out, beside] + rows
    straight = [between_cores(message) for message in rows]
    messages = messages[:2] + [message for pair in zip(rows, straight) for message in pair]
    shape = jax.ShapeDtypeStruct(displacement.shape, f32)
    return pl.pallas_call(
        lambda *refs: final_kernel(cols, len(row_perms), *refs),
        out_shape=(shape, shape),
        in_specs=[vmem()] * len(messages),
        out_specs=(vmem(), vmem()),
        compiler_params=limit(4),
        name="final",
    )(*messages)


def solution(mesh):
    in_specs = (P("sec", "row", None), P(None, "sec", "row", None), P(None, "sec", "row", None))
    out_specs = (P(None, "sec", "row", None), P(None, "sec", "row", None))
    return jax.shard_map(per_device, mesh=mesh, in_specs=in_specs, out_specs=out_specs, check_vma=False)
```

```python
import math

import jax
import jax.numpy as jnp
import numpy as np
from jax import lax
from jax.experimental import pallas as pl
from jax.experimental.pallas import tpu as pltpu
from jax.sharding import PartitionSpec as P

PATCH = 128
HALF = PATCH // 2
ITERS = 3
HALO = 3
WINDOW = 8
EXTRA = 16
PARTS = 8
FIRST_GROUP = 4
GROUP = 10

step_size = 0.5
stiffness = 0.2
epsilon = 1e-06
sharpness = 0.5 * PATCH
bf16 = jnp.bfloat16
f32 = jnp.float32


def split_table(table):
    table = np.asarray(table, np.float32)
    high = table.astype(bf16)
    low = (table - high.astype(np.float32)).astype(bf16)
    return high, low


def tables():
    n = PATCH
    index = np.arange(n)
    angle = 2.0 * np.pi / n * ((index[:, None] * index[None, :]) % n)
    cosine, sine = np.cos(angle), np.sin(angle)
    sign = 1.0 - 2.0 * (index % 2)

    basis = np.zeros((n, n))
    basis[:, :HALF] = cosine[:, :HALF]
    basis[:, HALF] = sign
    basis[:, HALF + 1 :] = -sine[:, 1:HALF]

    back = np.zeros((n, n))
    back[0] = 1.0
    back[1:HALF] = 2.0 * cosine[1:HALF]
    back[HALF] = sign
    back[HALF + 1 :] = -2.0 * sine[1:HALF]
    back /= n * n

    def doubled(table):
        pair = np.concatenate(split_table(table), axis=1)
        return np.concatenate([pair, pair], axis=0)

    down = np.concatenate(split_table(np.concatenate([cosine, -sine], axis=0)), axis=1)
    up = np.concatenate(split_table(np.concatenate([cosine, -sine], axis=1)), axis=0)
    return np.stack([doubled(basis), down, up]), doubled(back)


def split(values):
    high = values.astype(bf16)
    low = (values - high.astype(f32)).astype(bf16)
    return high, low


def dot(left, right):
    return jnp.dot(left, right, preferred_element_type=f32)


def fold(wide):
    return wide[:, :PATCH] + wide[:, PATCH:]


def side_by_side(left_high, left_low, rights):
    left = jnp.concatenate([left_high, left_low, left_high], axis=1)
    results = []
    for at in range(0, len(rights), 2):
        columns = []
        for right in rights[at : at + 2]:
            high, low = split(right)
            columns.append(jnp.concatenate([high, high, low], axis=0))
        wide = dot(left, jnp.concatenate(columns, axis=1))
        results += [wide[:, k * PATCH : (k + 1) * PATCH] for k in range(len(columns))]
    return results


def lanes(shape):
    return lax.broadcasted_iota(jnp.int32, shape, len(shape) - 1)


def alternating(shape, dim):
    return (1 - 2 * (lax.broadcasted_iota(jnp.int32, shape, dim) % 2)).astype(f32)


def half_of():
    return lax.rem(lax.axis_index("sec") + lax.axis_index("row"), 2)


def pack_kernel(shift_ref, mask_ref, image_ref, out_ref, shift, mask, sems):
    copies = [
        pltpu.make_async_copy(shift_ref, shift, sems.at[0]),
        pltpu.make_async_copy(mask_ref, mask, sems.at[1]),
    ]
    for part in range(PARTS):
        rows = pl.ds(part * (PATCH // PARTS), PATCH // PARTS)
        copies.append(pltpu.make_async_copy(image_ref.at[0, rows], out_ref.at[rows], sems.at[2 + part]))
    for copy in copies:
        copy.start()
    copies[0].wait()
    copies[1].wait()
    row = lax.broadcasted_iota(jnp.int32, (EXTRA, PATCH), 0)
    for col in range(shift_ref.shape[-1]):
        values = jnp.zeros((EXTRA, PATCH), f32)
        for dim in range(2):
            value = jnp.full((EXTRA, PATCH), shift[dim, 0, 0, col], f32)
            high = value.astype(bf16).astype(f32)
            middle = (value - high).astype(bf16).astype(f32)
            low = (value - high) - middle
            allowed = jnp.full((EXTRA, PATCH), mask[dim, 0, 0, col].astype(f32), f32)
            for at, part in enumerate((high, middle, low)):
                values = jnp.where(row == 3 * dim + at, part, values)
            values = jnp.where(row == 6 + dim, allowed, values)
        out_ref[PATCH:, col * PATCH : (col + 1) * PATCH] = values.astype(bf16)
    for copy in copies[2:]:
        copy.wait()


def forward_patches(patches, basis, down, mean_row):
    count = len(patches)
    rows = fold(dot(jnp.concatenate(patches, axis=0), basis))
    lane = lanes((1, PATCH))
    first_row = lax.broadcasted_iota(jnp.int32, (WINDOW, PATCH), 0) == 0
    sigma = jnp.where(lane > HALF, 1.0, -1.0) * jnp.where(lane % HALF == 0, 0.0, 1.0)
    pairs = []
    for k in range(count):
        row = rows[k * PATCH : (k + 1) * PATCH]
        part = jnp.sum(row.reshape(PATCH // WINDOW, WINDOW, PATCH), axis=0)
        whole = jnp.sum(part, axis=0, keepdims=True)
        row = row - (whole[:, :1] * (1.0 / (PATCH * PATCH))) * mean_row
        pair = jnp.concatenate(split(row), axis=1)
        pairs.append(jnp.concatenate([pair, pair], axis=0))
    both = [fold(dot(down, pair)) for pair in pairs]
    result = []
    for wide in both:
        first, second = wide[:PATCH], wide[PATCH:]
        real = first + sigma * pltpu.roll(second, HALF, 1)
        imag = second - sigma * pltpu.roll(first, HALF, 1)
        squares = (real * real + imag * imag).reshape(PATCH // WINDOW, WINDOW, PATCH)
        at = HALF // WINDOW
        energy = jnp.where(first_row, 0.0, squares[at])
        for k in range(PATCH // WINDOW):
            if k != at:
                energy = energy + squares[k]
        energy = jnp.sum(energy, axis=0, keepdims=True)
        result.append((real, imag, energy, real[HALF : HALF + 1], imag[HALF : HALF + 1]))
    return result


def slot_of(name):
    sec = lax.axis_index("sec")
    core = lax.rem(sec, 2)
    odd = lax.rem(sec // 2, 2)
    source, swapped = name
    if swapped:
        core = 1 - core
    if source == "own":
        return HALO + core
    if source == "a":
        return 5 - 4 * odd + core
    if source == "b":
        return 1 + 4 * odd + core
    return (WINDOW - 1) * core


def spectra_kernel(cols, names, pairs, starts, *refs):
    blocks, tables_ref = refs[: len(names)], refs[len(names)]
    basis_ref, down_ref, up_ref = [tables_ref.at[k] for k in range(3)]
    basis = basis_ref[:PATCH]
    ones = jnp.sum(basis.astype(f32), axis=0, keepdims=True)
    mean_row = ones[:, :PATCH] + ones[:, PATCH:]
    real_ref, imag_ref, row_ref, base_ref = refs[-4:]
    if starts:
        row_ref[...] = jnp.zeros(row_ref.shape, f32)
    half = half_of()
    slots = [slot_of(name) for name in names]
    places = [(block, slot, col) for block, slot in zip(blocks, slots) for col in range(cols)]
    starts = [pl.multiple_of((half * cols + col) * PATCH, PATCH) for col in range(cols)]
    patches = [block[:PATCH, pl.ds(starts[col], PATCH)] for block, slot, col in places]
    results = forward_patches(patches, basis, down_ref[...], mean_row)
    corner = (lax.broadcasted_iota(jnp.int32, (WINDOW, PATCH), 0) == 0) & (lanes((WINDOW, PATCH)) == HALF)
    for (block, slot, col), (real, imag, energy_row, nyquist_real, nyquist_imag) in zip(places, results):
        real_ref[slot, col] = real
        imag_ref[slot, col] = imag
        band = slice(HALF, HALF + WINDOW)
        real_ref[slot, col, band, :] = jnp.where(corner, 0.0, real[band])
        imag_ref[slot, col, band, :] = jnp.where(corner, 0.0, imag[band])
        row_ref[col, 0, pl.ds(slot, 1), :] = energy_row
        row_ref[col, 1, pl.ds(slot, 1), :] = nyquist_real
        row_ref[col, 11, pl.ds(slot, 1), :] = nyquist_imag
        small = block[PATCH:, pl.ds(starts[col], PATCH)].astype(f32)
        for dim in range(2):
            shift = small[3 * dim : 3 * dim + 1] + small[3 * dim + 1 : 3 * dim + 2] + small[3 * dim + 2 : 3 * dim + 3]
            row_ref[col, 2 + dim, pl.ds(slot, 1), :] = shift
            row_ref[col, 4 + dim, pl.ds(slot, 1), :] = small[6 + dim : 7 + dim]
    low_lane = lanes((1, PATCH)) <= HALF
    tasks = [(pair, col) for pair in pairs for col in range(cols)]
    for at in range(0, len(tasks), 2):
        products = []
        for pair, col in tasks[at : at + 2]:
            sr, si = real_ref[pair, col], imag_ref[pair, col]
            nr, ni = real_ref[pair + 1, col], imag_ref[pair + 1, col]
            same = sr * nr + si * ni
            cross = si * nr - sr * ni
            products.append(
                jnp.concatenate([jnp.where(low_lane, same, cross), jnp.where(low_lane, cross, -same)], axis=0)
            )
        for (pair, col), base in zip(tasks[at : at + 2], side_by_side(up_ref[:PATCH], up_ref[PATCH:], products)):
            base_ref[col, pair] = jnp.concatenate(split(base), axis=1)


def energies(row_ref, col):
    lane = lanes((WINDOW, PATCH))
    weight = jnp.where(lane == 0, 1.0, jnp.where(lane < HALF, 2.0, 0.0))
    at_nyquist = jnp.where(lane == HALF, 1.0, 0.0)
    area = float(PATCH * PATCH)

    def spread(values):
        return jnp.broadcast_to(jnp.sum(values, axis=1, keepdims=True), (WINDOW, PATCH))

    energy, real, imag = row_ref[col, 0], row_ref[col, 1], row_ref[col, 11]
    corner = spread(real * at_nyquist)
    row_energy = spread(weight * (real * real + imag * imag)) / area
    return spread(weight * energy) / area, row_energy, spread(energy * at_nyquist) / area, corner * corner / area, corner


def sine_cosine(z):
    zz = z * z
    sine = jnp.full_like(z, 1.0 / 6227020800.0)
    for factor in (-1.0 / 39916800.0, 1.0 / 362880.0, -1.0 / 5040.0, 1.0 / 120.0, -1.0 / 6.0, 1.0):
        sine = sine * zz + factor
    cosine = jnp.full_like(z, 1.0 / 479001600.0)
    for factor in (-1.0 / 3628800.0, 1.0 / 40320.0, -1.0 / 720.0, 1.0 / 24.0, -0.5, 1.0):
        cosine = cosine * zz + factor
    return sine * z, cosine


def cos_sin_turns(turns):
    sine, cosine = sine_cosine((turns - jnp.round(turns)) * math.pi)
    return 1.0 - 2.0 * sine * sine, 2.0 * sine * cosine


def shift_row(delta, gamma, lane):
    whole = jnp.round(delta)
    rest = delta - whole
    lag = lane.astype(f32) + whole
    lag = lag - PATCH * jnp.round(lag * (1.0 / PATCH))
    parity = (1 - 2 * (lag.astype(jnp.int32) & 1)).astype(f32)
    top, bottom = sine_cosine(rest * math.pi)
    sine, cosine = sine_cosine((lag + rest) * (math.pi / PATCH))
    centre = sine == 0.0
    ratio = jnp.where(centre, float(PATCH), top) / jnp.where(centre, 1.0, sine)
    nyquist = (1 - 2 * (lane & 1)).astype(f32) * gamma
    return (parity * (ratio * cosine - bottom) + nyquist) * (1.0 / PATCH)


def next_section(values):
    return pltpu.roll(values, WINDOW - 1, 0)


def previous_section(values):
    return pltpu.roll(values, 1, 0)


def column(message, lane):
    return jnp.broadcast_to(message[:, lane : lane + 1], (WINDOW, PATCH))


def pack_columns(values):
    lane = lanes((WINDOW, PATCH))
    packed = jnp.zeros((WINDOW, PATCH), f32)
    for at, value in enumerate(values):
        packed = jnp.where(lane == at, value, packed)
    return packed


def smoothed(updated, vertical, beside, half, cols):
    result = []
    for dim in range(2):
        current = []
        for col in range(cols):
            if col > 0:
                left = updated[dim][col - 1]
            else:
                left = jnp.where(half == 1, beside[dim][cols - 1], 0.0)
            if col < cols - 1:
                right = updated[dim][col + 1]
            else:
                right = jnp.where(half == 0, beside[dim][0], 0.0)
            own = updated[dim][col]
            current.append(own + stiffness * (left + right + vertical[dim][col] - 4.0 * own))
        result.append(current)
    return result


def unpack(message, cols, start=0):
    return [[column(message, start + dim * cols + col) for col in range(cols)] for dim in range(2)]


def add(left, right):
    return [[a + b for a, b in zip(x, y)] for x, y in zip(left, right)]


def iteration_kernel(cols, first, last, starts, n_vertical, *refs):
    base_ref, row_ref, back_ref = refs[:3]
    refs = refs[3:]
    core = lax.rem(lax.axis_index("sec"), 2)
    half = half_of()
    if starts:
        field = [[row_ref[col, 2 + dim] for col in range(cols)] for dim in range(2)]
    else:
        own_message, beside_message = refs[:2]
        vertical = unpack(refs[2][...], cols)
        for extra in refs[3 : 2 + n_vertical]:
            vertical = add(vertical, unpack(extra[...], cols))
        refs = refs[2 + n_vertical :]
        field = smoothed(unpack(own_message[...], cols), vertical, unpack(beside_message[...], cols), half, cols)
    out_ref, total_ref, moment_ref, edge_ref = refs
    lane = lanes((WINDOW, PATCH))
    frequency = (lane % HALF).astype(f32) * (1.0 / PATCH)
    high_lane = lane >= HALF
    nyquist_lane = lane == HALF
    zero_lane = lane % HALF == 0
    rows, turn_cos, turn_sin, ripple = [], [], [], []
    for col in range(cols):
        dy, dx = field[0][col], field[1][col]
        cos_y, sin_y = cos_sin_turns(dy * 0.5)
        cos_x, sin_x = cos_sin_turns(dx * 0.5)
        cos_both = cos_y * cos_x - sin_y * sin_x
        bulk, row_energy, col_energy, corner_energy, nyquist = [row_ref[col, 6 + k] for k in range(5)]
        energy = bulk + cos_y * cos_y * row_energy + cos_x * cos_x * col_energy + cos_both * cos_both * corner_energy
        scale = (sharpness / math.log(2.0)) / jnp.sqrt(energy * next_section(energy) + epsilon)
        gamma_y = cos_y * next_section(cos_y)
        gamma_x = cos_x * next_section(cos_x)
        gamma = cos_both * next_section(cos_both)
        corner = nyquist * next_section(nyquist) * (1.0 / (PATCH * PATCH))
        ripple.append(gamma * corner * scale)
        rows.append(shift_row(dy - next_section(dy), gamma_y, lane))
        cosine, sine = cos_sin_turns((dx - next_section(dx)) * frequency)
        turn_cos.append(jnp.where(nyquist_lane, gamma_x, cosine) * scale)
        turn_sin.append(jnp.where(zero_lane, 0.0, jnp.where(high_lane, -sine, sine)) * scale)
    checker = alternating((WINDOW, PATCH), 0) * alternating((WINDOW, PATCH), 1)
    blocks = PATCH // WINDOW
    block_order = [(blocks // 2 - 1 - k) % blocks for k in range(blocks)]
    row_in_block = lax.broadcasted_iota(jnp.int32, (WINDOW, PATCH), 0).astype(f32)
    for col in range(cols):
        total_ref[col] = jnp.ones((WINDOW, PATCH), f32)
        moment_ref[col] = jnp.zeros((WINDOW, PATCH), f32)
        edge_ref[col] = jnp.zeros((WINDOW, PATCH), f32)
    tasks = [(pair, col) for pair in range(first, last) for col in range(cols)]
    most = FIRST_GROUP if starts else GROUP
    size = -(-len(tasks) // -(-len(tasks) // most))
    for at in range(0, len(tasks), size):
        group = tasks[at : at + size]
        moved = []
        for pair, col in group:
            row = slice(pair, pair + 1)
            parts = [part.astype(f32) for part in split(rows[col][row])]
            parts = [
                pltpu.roll(jnp.broadcast_to(part, (PATCH, PATCH)), 0, 1, stride=1, stride_axis=0).astype(bf16)
                for part in parts
            ]
            base = base_ref[col, pair]
            moved.append(fold(dot(jnp.concatenate(parts, axis=1), jnp.concatenate([base, base], axis=0))))
        turned = []
        for (pair, col), value in zip(group, moved):
            row = slice(pair, pair + 1)
            value = value * turn_cos[col][row] + pltpu.roll(value, HALF, 1) * turn_sin[col][row]
            turned.append(jnp.concatenate(split(value), axis=1))
        wide = fold(dot(jnp.concatenate(turned, axis=0), back_ref[...]))
        for k, (pair, col) in enumerate(group):
            row = slice(pair, pair + 1)
            scores = wide[k * PATCH : (k + 1) * PATCH].reshape(blocks, WINDOW, PATCH)
            weights = jnp.exp2(scores + (ripple[col][row] * checker)[None])
            total = weights[block_order[0]]
            moment = total
            for m in block_order[1:-1]:
                total = total + weights[m]
                moment = moment + total
            total = total + weights[block_order[-1]]
            moment = float(WINDOW) * moment + (row_in_block - PATCH // 2) * total
            total_ref[col, row, :] = jnp.sum(total, axis=0, keepdims=True)
            moment_ref[col, row, :] = jnp.sum(moment, axis=0, keepdims=True)
            edge_ref[col, row, :] = weights[blocks // 2, 0:1]
    sec_total = lax.axis_size("sec")
    section = lax.broadcasted_iota(jnp.int32, (WINDOW, PATCH), 0) + (lax.axis_index("sec") - core - HALO)
    lag = jnp.where(high_lane, lane - PATCH, lane).astype(f32)

    def spread(values):
        return jnp.broadcast_to(jnp.sum(values, axis=1, keepdims=True), (WINDOW, PATCH))

    updated = [[None] * cols for _ in range(2)]
    averaged = [[None] * cols for _ in range(2)]
    for col in range(cols):
        total = total_ref[col]
        inverse = 1.0 / spread(total)
        offsets = (spread(moment_ref[col]) * inverse, spread(total * lag) * inverse)
        edges = (spread(edge_ref[col]) * inverse, spread(jnp.where(nyquist_lane, total, 0.0)) * inverse)
        lower = row_ref[col, 4] * (section > 0).astype(f32)
        upper = row_ref[col, 5] * (section < sec_total - 1).astype(f32)
        for dim in range(2):
            reverse = previous_section(-(offsets[dim] + float(PATCH) * edges[dim]))
            mean = (lower * reverse + upper * offsets[dim]) / jnp.maximum(lower + upper, 1.0)
            averaged[dim][col] = mean
            updated[dim][col] = field[dim][col] + step_size * mean
    flat = [updated[dim][col] for dim in range(2) for col in range(cols)]
    flat += [averaged[dim][col] for dim in range(2) for col in range(cols)]
    out_ref[...] = pack_columns(flat)


def final_kernel(cols, n_vertical, *refs):
    own, beside = refs[0][...], refs[1][...]
    vertical = unpack(refs[2][...], cols)
    vertical_beside = unpack(refs[3][...], cols)
    for k in range(1, n_vertical):
        vertical = add(vertical, unpack(refs[2 + 2 * k][...], cols))
        vertical_beside = add(vertical_beside, unpack(refs[3 + 2 * k][...], cols))
    field_ref, mean_ref = refs[2 + 2 * n_vertical :]
    core = lax.rem(lax.axis_index("sec"), 2)
    mine, other = unpack(own, cols), unpack(beside, cols)
    half = half_of()
    here = smoothed(mine, vertical, other, half, cols)
    there = smoothed(other, vertical_beside, mine, 1 - half, cols)
    mean_here, mean_there = unpack(own, cols, 2 * cols), unpack(beside, cols, 2 * cols)
    lane = lanes((1, PATCH))

    def pick(values):
        return jnp.where(core == 0, values[HALO : HALO + 1], values[HALO + 1 : HALO + 2])

    for out, a, b in ((field_ref, here, there), (mean_ref, mean_here, mean_there)):
        for dim in range(2):
            row = jnp.zeros((1, PATCH), f32)
            for col in range(cols):
                first = pick(jnp.where(half == 0, a[dim][col], b[dim][col]))
                second = pick(jnp.where(half == 0, b[dim][col], a[dim][col]))
                row = jnp.where(lane == col, first, row)
                row = jnp.where(lane == cols + col, second, row)
            out[dim, 0] = row[:, : 2 * cols]


def limit(mebibytes):
    return pltpu.CompilerParams(vmem_limit_bytes=mebibytes << 20)


def anywhere():
    return pl.BlockSpec(memory_space=pl.ANY)


def vmem():
    return pl.BlockSpec(memory_space=pltpu.VMEM)


def swap(pairs):
    return [(a, b) for a, b in pairs] + [(b, a) for a, b in pairs]


def per_device(section_images, displacement, fold_mask):
    n_sec, n_row = lax.axis_size("sec"), lax.axis_size("row")
    patch_cols = displacement.shape[-1]
    assert patch_cols % 2 == 0 and n_sec % 2 == 0
    assert section_images.shape[:2] == (1, PATCH)
    cols = patch_cols // 2
    chips = n_sec // 2
    spectrum_tables, back_table = [jnp.asarray(table) for table in tables()]

    def sections(pairs):
        return [(2 * a + c, 2 * b + c) for a, b in pairs for c in range(2)]

    swap_a = sections(swap([(j, j + 1) for j in range(0, chips - 1, 2)]))
    swap_b = sections(swap([(j, j + 1) for j in range(1, chips - 1, 2)]))
    far = swap([(2 * j + 1, 2 * j + 4) for j in range(chips - 2)])
    cores = swap([(2 * j, 2 * j + 1) for j in range(chips)])

    def between_cores(x):
        return lax.ppermute(x, "sec", cores)

    payload = pl.pallas_call(
        pack_kernel,
        out_shape=jax.ShapeDtypeStruct((PATCH + EXTRA, patch_cols * PATCH), bf16),
        in_specs=[anywhere()] * 3,
        out_specs=vmem(),
        scratch_shapes=[
            pltpu.SMEM(displacement.shape, f32),
            pltpu.SMEM(fold_mask.shape, jnp.int32),
            pltpu.SemaphoreType.DMA((2 + PARTS,)),
        ],
        compiler_params=limit(4),
        cost_estimate=pl.CostEstimate(flops=0, bytes_accessed=8000000, transcendentals=0),
        name="pack",
    )(*[pltpu.with_memory_space_constraint(x, pltpu.HBM) for x in (displacement, fold_mask, section_images)])
    blocks = {("own", 0): payload}
    for source, perm in (("a", swap_a), ("b", swap_b), ("far", far)):
        blocks[source, 0] = lax.ppermute(payload, "sec", perm)
    for source in ("own", "a", "b", "far"):
        blocks[source, 1] = between_cores(blocks[source, 0])
    state = []
    row_perms = [swap([(r, r + 1) for r in range(0, n_row - 1, 2)])]
    if n_row > 2:
        row_perms.append(swap([(r, r + 1) for r in range(1, n_row - 1, 2)]))
    every = tuple(range(WINDOW - 1))
    stages = (
        ((("own", 0), ("own", 1)), (HALO,)),
        ((("a", 0),), ()),
        ((("a", 1), ("b", 0), ("far", 0)), ()),
        ((("b", 1), ("far", 1)), every[:HALO] + every[HALO + 1 :]),
    )
    state_shapes = [
        jax.ShapeDtypeStruct((WINDOW, cols, PATCH, PATCH), f32),
        jax.ShapeDtypeStruct((WINDOW, cols, PATCH, PATCH), f32),
        jax.ShapeDtypeStruct((cols, 12, WINDOW, PATCH), f32),
        jax.ShapeDtypeStruct((cols, WINDOW - 1, PATCH, 2 * PATCH), bf16),
    ]
    message_shape = jax.ShapeDtypeStruct((WINDOW, PATCH), f32)
    sums = [pltpu.VMEM((cols, WINDOW, PATCH), f32)] * 3
    for stage, (names, pairs) in enumerate(stages):
        last = stage == len(stages) - 1
        operands = [blocks[name] for name in names] + [spectrum_tables]

        def stage_kernel(*refs, names=names, pairs=pairs, stage=stage, last=last):
            if not last:
                spectra_kernel(cols, names, pairs, stage == 0, *refs)
                return
            count = len(names) + 1
            outs = refs[count + 5 :]
            spectra_kernel(cols, names, pairs, False, *refs[:count], *outs[:4])
            for col in range(cols):
                for k, value in enumerate(energies(outs[2], col)):
                    outs[2][col, 6 + k] = value
            iteration_kernel(cols, 0, WINDOW - 1, True, 0, outs[3], outs[2], refs[count], *outs[4:])

        first_alias = len(operands) + last
        state = pl.pallas_call(
            stage_kernel,
            out_shape=state_shapes + [message_shape] * last,
            in_specs=[vmem()] * (first_alias + len(state)),
            out_specs=[vmem()] * (4 + last),
            scratch_shapes=sums * last,
            input_output_aliases={first_alias + k: k for k in range(len(state))},
            compiler_params=limit(16),
            cost_estimate=pl.CostEstimate(flops=500000000, bytes_accessed=1000000, transcendentals=0),
            name="spectra",
        )(*operands, *[back_table] * last, *state)
    base, stats, out = state[3], state[2], state[4]

    def diagonal(x, rows):
        pairs = [(s * n_row + a, t * n_row + b) for s, t in cores for a, b in rows]
        return lax.ppermute(x, ("sec", "row"), pairs)

    messages = []
    for step in range(ITERS):
        if step > 0:
            out = pl.pallas_call(
                lambda *refs, step=step: iteration_kernel(cols, step, WINDOW - 1 - step, False, len(row_perms), *refs),
                out_shape=message_shape,
                in_specs=[vmem()] * (3 + len(messages)),
                out_specs=vmem(),
                scratch_shapes=sums,
                compiler_params=limit(8),
                name="iteration",
            )(base, stats, back_table, *messages)
        beside = between_cores(out)
        rows = [diagonal(out, perm) for perm in row_perms]
        messages = [out, beside] + rows
    straight = [between_cores(message) for message in rows]
    messages = messages[:2] + [message for pair in zip(rows, straight) for message in pair]
    shape = jax.ShapeDtypeStruct(displacement.shape, f32)
    return pl.pallas_call(
        lambda *refs: final_kernel(cols, len(row_perms), *refs),
        out_shape=(shape, shape),
        in_specs=[vmem()] * len(messages),
        out_specs=(vmem(), vmem()),
        compiler_params=limit(4),
        name="final",
    )(*messages)


def solution(mesh):
    in_specs = (P("sec", "row", None), P(None, "sec", "row", None), P(None, "sec", "row", None))
    out_specs = (P(None, "sec", "row", None), P(None, "sec", "row", None))
    return jax.shard_map(per_device, mesh=mesh, in_specs=in_specs, out_specs=out_specs, check_vma=False)
```
